256 devices in a mesh: dp: 32 (over x, z), tensor: 8 (over y, core).
Axes of the slice: x: 4, y: 4, z: 8, core: 2. Of those that a mesh axis runs over, the one named last changes fastest.
Arguments:
- activations: bfloat16 [2048, 24, 14336], P('dp', None, 'tensor'), may hold values from -6 to 6
- out_grads: bfloat16 [2048, 24, 4096], P('dp', None, 'tensor'), may hold values from -6 to 6
- proj_in: bfloat16 [14336, 64], P('tensor'), may hold values from -0.046875 to 0.046875
- proj_out: bfloat16 [4096, 64], P('tensor'), may hold values from -0.09375 to 0.09375
- queries: bfloat16 [32, 5120, 4096], P('dp', 'tensor'), may hold values from -0.09375 to 0.09375
- candidates: int32 [2048, 4], P('dp'), may hold values from 0 to 31, all different within a row; in each aligned block of 64 rows (0 to 63, 64 to 127, ...) at most 20 rows name the same one
Outputs:
- scores: float32 [2048, 4, 5120], P('dp', None, 'tensor')
The draws below stay inside these ranges and needn't reach their ends.
Inputs may be any that keep to these rules, and one draw needn't show every extreme that they name: `candidates`: each example names 4 different groups. Among the 64 examples of one index of dp at most 20 name the same group, and in every draw some group is named by exactly 20 of them.
All inputs are finite; a program needn't handle non-finite values.
Results may differ from the reference program's by a relative error of at most 0.0029.
Values may be sent and summed in bfloat16 or wider, within the bound.
A program may use at most 64 MiB of HBM per device.

```python
import math
import jax
import jax.numpy as jnp
import numpy as np
from jax import lax

D = 4096
FF = 14336
R = 64
T_EX = 24
EX_DEV = 64
GRAD = 4096
CANDS = 4
CAP = 20
EXAMPLES = 2048
GROUPS = 32
QN = 5120
N_DP = 32


def level_of(rng, extent, pieces, smallest, largest):
    def one(axis_at, shards_of):
        heights = jax.random.uniform(jax.random.fold_in(jax.random.fold_in(rng, 6), axis_at), (shards_of,), jnp.float32, smallest / len(pieces), largest / len(pieces))
        return jnp.repeat(jnp.exp(heights), extent[axis_at] // shards_of).reshape((-1,) + (1,) * (len(extent) - axis_at - 1))

    gain = one(*pieces[0])
    for cut in pieces[1:]:
        gain = gain * one(*cut)
    return gain


def routed_block(own_key, own, number, rows, number_of, top, bound, skew):
    order = jax.random.permutation(own_key, number_of)
    packed, common = portions_of(number_of, rows * top, bound, skew, True), portions_of(number_of, rows * top, bound, skew, False)
    places = jnp.arange(number_of)

    def named(lengths, rotation):
        used = int((lengths > 0).sum())
        fixed = max(1, used // 4)
        moved = fixed + (places - fixed + rotation * (used - fixed)) % max(1, number_of - fixed)
        return jnp.zeros((number_of,), jnp.int32).at[order[jnp.where(places < fixed, places, moved)]].set(jnp.asarray(lengths, jnp.int32))

    lengths = jnp.where(number % 4 == 0, named(packed, number // 4), named(common, number - number // 4 - 1))
    mixed = jax.random.permutation(jax.random.fold_in(own, 3), number_of)
    donor, receiver = mixed[0:number_of // 2 * 2:2], mixed[1:number_of // 2 * 2:2]
    room = jnp.minimum(lengths[donor] - 1, bound - lengths[receiver]) // 2
    room = jnp.where((donor == order[0]) | (receiver == order[0]) | (lengths[receiver] == 0), 0, jnp.maximum(room, 0))
    moved = jax.random.randint(jax.random.fold_in(own, 4), (number_of // 2,), 0, 1 << 20) % (room + 1)
    lengths = lengths.at[donor].add(-moved).at[receiver].add(moved)
    members = jnp.searchsorted(jnp.cumsum(lengths), jnp.arange(rows * top), side="right").astype(jnp.int32)
    table = members.reshape(top, rows).T
    table = table[jax.random.permutation(jax.random.fold_in(own, 1), rows)]
    rotation = jax.random.randint(jax.random.fold_in(own, 2), (rows, 1), 0, top)
    return jnp.take_along_axis(table, (jnp.arange(top)[None, :] + rotation) % top, axis=1)


def portions_of(number_of, total, most, slope, full):
    weights = [(1 << 20) // math.isqrt(rank ** slope) + 1 for rank in range(1, number_of + 1)]
    largest = most if full else min(most, max(-(-total // number_of), total * weights[0] // sum(weights)))
    least = 1 if total - largest >= number_of - 1 else 0
    holding, surplus = [largest] + [least] * (number_of - 1), total - largest - least * (number_of - 1)
    while surplus > 0:
        movable = [i for i in range(1, number_of) if holding[i] < largest] or [i for i in range(1, number_of) if holding[i] < most]
        whole, remaining = sum([weights[i] for i in movable]), surplus
        for i in movable:
            addition = min(most - holding[i], max(1, remaining * weights[i] // whole), surplus)
            holding[i] = holding[i] + addition
            surplus = surplus - addition
    return np.array(holding)


def bell_draw(key, dims, spread, reach, pieces=(), held_as=jnp.bfloat16):
    level = level_of(key, dims, pieces, -0.22, 0.18) if pieces else 1.0
    entries = jax.random.normal(key, dims, jnp.float32) * spread * level
    return jnp.minimum(jnp.maximum(entries, -reach), reach).astype(held_as)


def setup_inputs(seed: int = 0) -> dict:
    splits = jax.random.split(jax.random.key(seed), 7)
    activations = bell_draw(splits[0], (EXAMPLES, T_EX, FF), 1.0, 6.0, ((0, 32), (2, 8)))
    out_grads = bell_draw(splits[1], (EXAMPLES, T_EX, D), 1.0, 6.0, ((0, 32), (2, 8)))
    proj_in = bell_draw(splits[2], (FF, R), FF ** -0.5, 0.046875, ((0, 8),))
    proj_out = bell_draw(splits[3], (D, R), D ** -0.5, 0.09375, ((0, 8),))
    queries = bell_draw(splits[4], (GROUPS, QN, GRAD), GRAD ** -0.5, 0.09375, ((0, 32), (1, 8)))
    candidates_keys = jax.random.split(jax.random.fold_in(splits[5], 1), EXAMPLES // EX_DEV)
    candidates_turns = jax.random.permutation(jax.random.fold_in(splits[5], 3), EXAMPLES // EX_DEV)
    candidates = jax.vmap(lambda own, number: routed_block(jax.random.fold_in(splits[5], 2), own, number, EX_DEV, N_DP, CANDS, CAP, 2))(candidates_keys, candidates_turns).reshape((EXAMPLES, CANDS))
    return {"activations": activations, "out_grads": out_grads, "proj_in": proj_in, "proj_out": proj_out, "queries": queries, "candidates": candidates}


epsilon = 1e-06

def reference(activations, out_grads, proj_in, proj_out, queries, candidates):
    row_count = EXAMPLES * T_EX
    act_proj = jnp.dot(activations.reshape(row_count, FF), proj_in, preferred_element_type=jnp.float32).reshape(EXAMPLES, T_EX, R)
    grad_proj = jnp.dot(out_grads.reshape(row_count, D), proj_out, preferred_element_type=jnp.float32).reshape(EXAMPLES, T_EX, R)
    example_grads = jnp.einsum('eta,etb->eab', grad_proj, act_proj, precision=lax.Precision.HIGHEST).reshape(EXAMPLES, GRAD)
    inv_rms = lax.rsqrt(lax.optimization_barrier(jnp.mean(example_grads * example_grads, axis=1, keepdims=True)) + epsilon)
    unit_grads = (example_grads * inv_rms).astype(jnp.bfloat16)
    flat_cands = candidates.reshape(-1).astype(jnp.int32)
    pair_count = EXAMPLES * CANDS
    sorted_pairs = jnp.argsort(flat_cands, stable=True).astype(jnp.int32)
    counts = lax.optimization_barrier(jnp.sum((flat_cands[:, None] == jnp.arange(GROUPS, dtype=jnp.int32)[None, :]).astype(jnp.int32), axis=0)).astype(jnp.int32)
    starts = (jnp.cumsum(counts) - counts).astype(jnp.int32)
    pad_rows = N_DP * CAP
    padded = jnp.concatenate([sorted_pairs, jnp.zeros((pad_rows,), jnp.int32)])

    def visit_group(group, all_scores):
        pair_ids = lax.dynamic_slice(padded, (starts[group].astype(jnp.int32),), (pad_rows,))
        is_live = jnp.arange(pad_rows, dtype=jnp.int32) < counts[group]
        group_queries = lax.dynamic_index_in_dim(queries, group, 0, keepdims=False)
        group_scores = jnp.dot(unit_grads[pair_ids // CANDS], group_queries.T, preferred_element_type=jnp.float32)
        target = jnp.where(is_live, pair_ids, pair_count).astype(jnp.int32)
        return all_scores.at[target].set(group_scores, mode='drop')
    all_scores = lax.fori_loop(0, GROUPS, visit_group, jnp.zeros((pair_count, QN), jnp.float32))
    return all_scores.reshape(EXAMPLES, CANDS, QN)
```

```python
import jax
import jax.numpy as jnp
from jax import lax
from jax.experimental import pallas as pl
from jax.experimental.pallas import tpu as pltpu
from jax.sharding import PartitionSpec as P

EPS = 1e-06
NX, NZ, NY = 4, 8, 4
F32, BF16, I32 = jnp.float32, jnp.bfloat16, jnp.int32
NT = (((1,), (1,)), ((), ()))


def iota(shape, axis):
    return lax.broadcasted_iota(I32, shape, axis)


def main_kernel(
    act, og, pin, pout, qh, cand, ret,
    abuf, obuf, wa, wo, expand, part, rcore, csum, rrel, fin, rfin, pbuf, ubuf32, usend,
    zb, xs, r, q0, q1, rs,
    act_sem, og_sem, q_sem,
    core_s, core_r, rel_s, rel_r, fin_s, fin_r, u_s, u_r,
    z_s, z_r, x_s, x_r, y_s, y_r, c_s, c_r, b_s, b_r,
):
    dp = lax.axis_index("dp")
    t = lax.axis_index("tensor")
    x, z = dp // NZ, dp % NZ
    y, c = t // 2, t % 2

    def dev(dp_to, t_to):
        return {"dp": dp_to, "tensor": t_to}

    def rcopy(src, dst, ss, rr, to):
        return pltpu.make_async_remote_copy(
            src_ref=src, dst_ref=dst, send_sem=ss, recv_sem=rr,
            device_id=to, device_id_type=pl.DeviceIdType.MESH,
        )

    partner = dev(dp, 2 * y + (1 - c))
    yup = dev(dp, 2 * ((y + 1) % NY) + c)
    ydn = dev(dp, 2 * ((y + NY - 1) % NY) + c)
    zup = dev(x * NZ + (z + 1) % NZ, t)
    zdn = dev(x * NZ + (z + NZ - 1) % NZ, t)

    ys = [(y + 2) % NY, (y + 1) % NY, (y + 3) % NY, y]
    loads = []
    for n in range(8):
        tb = 2 * ys[n // 2] + ((1 - c) if n % 2 == 0 else c)
        rows = pl.ds(pl.multiple_of(tb * 192, 192), 192)
        a = pltpu.make_async_copy(act.at[rows, :], abuf.at[n], act_sem.at[n])
        o = pltpu.make_async_copy(og.at[rows, :], obuf.at[n], og_sem.at[n])
        a.start()
        o.start()
        loads.append((a, o))

    barrier = pltpu.get_barrier_semaphore()

    @pl.loop(1, NX * NZ)
    def _(k):
        pl.semaphore_signal(barrier, inc=1, device_id=dev((dp + k) % (NX * NZ), t),
                            device_id_type=pl.DeviceIdType.MESH)

    @pl.loop(1, 8)
    def _(k):
        pl.semaphore_signal(barrier, inc=1, device_id=dev(dp, (t + k) % 8),
                            device_id_type=pl.DeviceIdType.MESH)

    rel_y = [y, (y + 3) % NY, (y + 1) % NY, (y + 2) % NY]
    qloads = []
    for rel in range(8):
        ts = 2 * rel_y[rel // 2] + (c if rel % 2 == 0 else 1 - c)
        for h, dst in ((0, q0), (1, q1)):
            cols = pl.ds(pl.multiple_of(ts * 512 + h * 256, 256), 256)
            cp = pltpu.make_async_copy(
                qh.at[:, cols], dst.at[:, pl.ds(rel * 256, 256)], q_sem.at[2 * rel + h]
            )
            cp.start()
            qloads.append(cp)

    wa[0:64, :] = jnp.zeros((64, wa.shape[1]), BF16)
    wa[64:128, :] = pin[...]
    wo[0:64, :] = pout[...]
    wo[64:128, :] = jnp.zeros((64, wo.shape[1]), BF16)

    def project(n):
        for cp in loads[n]:
            cp.wait()
        part[n] = lax.dot_general(
            abuf[n], wa[...], NT, preferred_element_type=F32
        ) + lax.dot_general(obuf[n], wo[...], NT, preferred_element_type=F32)

    core_cp = [rcopy(part.at[2 * j], rcore.at[j], core_s.at[j], core_r.at[j], partner)
               for j in range(4)]
    rel_cp = [rcopy(csum.at[pl.ds(0, 96)], rrel.at[0], rel_s.at[0], rel_r.at[0], yup),
              rcopy(csum.at[pl.ds(96, 96)], rrel.at[1], rel_s.at[1], rel_r.at[1], ydn)]
    fin_cp = [rcopy(fin.at[0], rfin.at[0], fin_s.at[0], fin_r.at[0], yup),
              rcopy(fin.at[1], rfin.at[1], fin_s.at[1], fin_r.at[1], ydn)]

    project(0)
    pl.semaphore_wait(barrier, NX * NZ - 1 + 7)
    core_cp[0].start()
    project(1)
    project(2)
    core_cp[1].start()
    project(3)
    core_cp[0].wait_recv()
    csum[...] = part[1] + rcore[0]
    rel_cp[0].start()
    rel_cp[1].start()
    project(4)
    core_cp[2].start()
    project(5)
    project(6)
    core_cp[3].start()
    project(7)

    row = iota((256, 4096), 0)
    col = iota((256, 4096), 1)
    expand[...] = jnp.where((row % 64 == col // 64) & (row < 192), 1.0, 0.0).astype(BF16)
    e_of = iota((64, 128), 1) // 16 * 8 + iota((64, 128), 1) % 8
    dup = jnp.where(iota((64, 128), 0) == e_of, 1.0, 0.0).astype(BF16)
    c2 = jnp.dot(cand[...].astype(F32).astype(BF16), dup, preferred_element_type=F32)
    zb[0, 128:136, 0:128] = c2.astype(BF16)
    zb[0, 128:136, 128:256] = jnp.zeros((8, 128), BF16)

    core_cp[1].wait_recv()
    rel_cp[0].wait_recv()
    fin[0, 0:96] = part[3, 0:96] + rcore[1, 0:96] + rrel[0]
    fin[0, 96:192] = part[3, 96:192] + rcore[1, 96:192]
    fin_cp[0].start()
    core_cp[2].wait_recv()
    rel_cp[1].wait_recv()
    fin[1, 0:96] = part[5, 0:96] + rcore[2, 0:96]
    fin[1, 96:192] = part[5, 96:192] + rcore[2, 96:192] + rrel[1]
    fin_cp[1].start()
    core_cp[3].wait_recv()
    fin_cp[0].wait_recv()
    fin_cp[1].wait_recv()
    pbuf[...] = part[7] + rcore[3] + rfin[0] + rfin[1]

    pt = jnp.concatenate([pbuf[pl.ds(k, 8, stride=24), :] for k in range(24)], axis=0)
    lane = iota((192, 128), 1)
    low = lane < 64
    a2 = jnp.where(low, pltpu.roll(pt, 64, 1), pt)
    a4 = jnp.concatenate([a2, a2], axis=1)
    hi = pt.astype(BF16).astype(F32)
    rest = pt - hi
    mid = rest.astype(BF16).astype(F32)
    lo = rest - mid
    g3 = jnp.concatenate(
        [jnp.where(low, hi, pltpu.roll(mid, 64, 1)), jnp.where(low, lo, 0.0)], axis=1
    ).astype(BF16)
    sq = jnp.zeros((8, 256), F32)
    for m in range(16):
        gx = jnp.dot(g3, expand[:, 256 * m:256 * m + 256], preferred_element_type=F32)
        u = jnp.sum((gx * a4).reshape(24, 8, 256), axis=0)
        ubuf32[:, 256 * m:256 * m + 256] = u
        sq = sq + u * u
    inv = lax.rsqrt(jnp.sum(sq, axis=1, keepdims=True) / 4096.0 + EPS)
    for m in range(16):
        usend[m // 2, 8 * (m % 2):8 * (m % 2) + 8, :] = (
            ubuf32[:, 256 * m:256 * m + 256] * inv
        ).astype(BF16)
    my_rows = pl.ds(pl.multiple_of(t * 16, 16), 16)
    u_cp = []
    for k in range(1, 8):
        to = (t + k) % 8
        u_cp.append(rcopy(usend.at[to], zb.at[0, my_rows, :], u_s.at[k], u_r.at[k], dev(dp, to)))
        u_cp[-1].start()
    zb[0, my_rows, :] = usend[t]

    def u_in(k):
        fr = (t + 8 - k) % 8
        return rcopy(usend.at[fr], zb.at[0, pl.ds(pl.multiple_of(fr * 16, 16), 16), :],
                     u_s.at[k], u_r.at[k], dev(dp, fr))

    tri_r, tri_c = iota((128, 128), 0), iota((128, 128), 1)
    tri = jnp.where(
        ((tri_r // 8) % 2 == 0)
        & (tri_r // 16 * 8 + tri_r % 8 < tri_c // 16 * 8 + tri_c % 8), 1.0, 0.0
    ).astype(BF16)
    mr = iota((40, 128), 0)
    slot_of = jnp.where(mr < 16, mr, jnp.where(mr < 20, mr, jnp.where(mr < 24, mr - 4, mr - 24)))
    half_of = jnp.where(mr < 20, 0, 1)
    rowkey = (slot_of + 64 * half_of).astype(F32)
    half_lane = ((iota((1, 128), 1) // 8) % 2 * 64).astype(F32)

    for k in range(1, 8):
        u_in(k).wait_recv()
    for cp in qloads:
        cp.wait()

    def z_in(d):
        return rcopy(zb.at[d], zb.at[d], z_s.at[d], z_r.at[d], zup)

    z_half = [rcopy(zb.at[3, pl.ds(0, 72)], zb.at[4, pl.ds(0, 72)], z_s.at[4], z_r.at[4], zup),
              rcopy(zb.at[5, pl.ds(72, 64)], zb.at[4, pl.ds(72, 64)], z_s.at[0], z_r.at[0], zdn)]

    def z_up(d):
        return rcopy(zb.at[d], zb.at[d + 1], z_s.at[d + 1], z_r.at[d + 1], zup)

    def z_dn(d):
        n = (d + 7) % 8
        return rcopy(zb.at[d], zb.at[n], z_s.at[n], z_r.at[n], zdn)

    z_up(0).start()
    z_dn(0).start()

    def piece(i):
        half = (i + 1) // 2
        return (half * (2 * (i % 2) - 1) + 8) % 8

    def x_cp(d, k):
        return rcopy(xs.at[d, k], r.at[0, d, k], x_s.at[d, k], x_r.at[d, k],
                     dev((x + k) % NX * NZ + z, t))

    def y_cp(d, k):
        if k == 0:
            return rcopy(r.at[0, d], r.at[2, d], y_s.at[d, 0], y_r.at[d, 0], yup)
        if k == 1:
            return rcopy(r.at[0, d], r.at[4, d], y_s.at[d, 1], y_r.at[d, 1], ydn)
        if k == 2:
            return rcopy(r.at[2, d, pl.ds(0, 2)], r.at[6, d, pl.ds(0, 2)],
                         y_s.at[d, 2], y_r.at[d, 2], yup)
        return rcopy(r.at[4, d, pl.ds(2, 2)], r.at[6, d, pl.ds(2, 2)],
                     y_s.at[d, 3], y_r.at[d, 3], ydn)

    def c_cp(d, k):
        return rcopy(r.at[2 * k, d], r.at[2 * k + 1, d], c_s.at[d, k], c_r.at[d, k], partner)

    def b_cp(d, k):
        to = (x + NX - k) % NX * NZ + (z + NZ - d) % NZ
        return rcopy(rs.at[d, k], ret.at[d, k], b_s.at[d, k], b_r.at[d, k], dev(to, t))

    def own_cp():
        return pltpu.make_async_copy(rs.at[0, 0], ret.at[0, 0], b_s.at[0, 0])

    def pack(d):
        cz = zb[d, 128:136, 0:128].astype(F32)
        eqs = []
        for k in range(NX):
            g = ((x + k) % NX * NZ + z).astype(F32)
            eqs.append(jnp.where(cz == g, 1.0, 0.0))
        ranks = jnp.dot(jnp.concatenate(eqs, axis=0).astype(BF16), tri,
                        preferred_element_type=F32)
        hots = []
        for k in range(NX):
            hit = jnp.sum(eqs[k], axis=0, keepdims=True)
            rank = jnp.sum(ranks[8 * k:8 * k + 8], axis=0, keepdims=True)
            key = jnp.where(hit > 0.5, rank + half_lane, -1.0)
            hots.append(jnp.where(rowkey == key, 1.0, 0.0))
        hot = jnp.concatenate(hots, axis=0).astype(BF16)
        msg = jnp.dot(hot, zb[d, 0:128, :], preferred_element_type=F32)
        r[0, d, 0] = msg[0:40].astype(BF16)
        for k in range(1, NX):
            xs[d, k] = msg[40 * k:40 * k + 40].astype(BF16)

    row8 = iota((8, 128), 0)

    def scores(d):
        l0 = jnp.concatenate([r[k, d, :, 0:24, :].reshape(96, 256) for k in range(8)], axis=1)
        l1 = jnp.concatenate([r[k, d, :, 16:40, :].reshape(96, 256) for k in range(8)], axis=1)
        acc0 = lax.dot_general(l0, q0[...], NT, preferred_element_type=F32)
        acc1 = lax.dot_general(l1, q1[...], NT, preferred_element_type=F32)
        for k in range(NX):
            b = 24 * k
            m = acc0[b:b + 16] + acc1[b + 8:b + 24]
            ex = acc0[b + 16:b + 24] + pltpu.roll(acc1[b:b + 8], 4, 0)
            ex2 = pltpu.roll(ex, 4, 0)
            for j in range(5):
                rs[d, k, 16 * j:16 * j + 16, :] = m[:, 128 * j:128 * j + 128].astype(BF16)
            for j in range(3):
                v = ex[:, 128 * j:128 * j + 128]
                if j < 2:
                    v = jnp.where(row8 < 4, v, ex2[:, 128 * j + 384:128 * j + 512])
                rs[d, k, 80 + 8 * j:88 + 8 * j, :] = v.astype(BF16)

    @pl.loop(0, 12)
    def _(i):
        @pl.when(i < 8)
        def _():
            d = piece(i)

            @pl.when((i % 2 == 1) & (i < 7))
            def _():
                z_in(d).wait_recv()

                @pl.when(d < 3)
                def _():
                    z_up(d).start()

                @pl.when(d == 3)
                def _():
                    z_half[0].start()

            @pl.when((i % 2 == 0) & (i > 0))
            def _():
                z_in(d).wait_recv()

                @pl.when(d > 5)
                def _():
                    z_dn(d).start()

                @pl.when(d == 5)
                def _():
                    z_half[1].start()

            @pl.when(i == 7)
            def _():
                z_half[0].wait_recv()
                z_half[1].wait_recv()

            pack(d)
            for k in range(1, NX):
                x_cp(d, k).start()

        @pl.when((i >= 1) & (i < 9))
        def _():
            d = piece(i - 1)
            for k in range(1, NX):
                x_cp(d, k).wait_recv()
            y_cp(d, 0).start()
            y_cp(d, 1).start()
            c_cp(d, 0).start()

        @pl.when((i >= 2) & (i < 10))
        def _():
            d = piece(i - 2)
            y_cp(d, 0).wait_recv()
            y_cp(d, 2).start()
            y_cp(d, 1).wait_recv()
            y_cp(d, 3).start()
            c_cp(d, 1).start()
            c_cp(d, 2).start()

        @pl.when((i >= 3) & (i < 11))
        def _():
            d = piece(i - 3)
            y_cp(d, 2).wait_recv()
            y_cp(d, 3).wait_recv()
            c_cp(d, 3).start()

        @pl.when(i >= 4)
        def _():
            d = piece(i - 4)
            for k in range(4):
                c_cp(d, k).wait_recv()
            scores(d)
            for k in range(1, NX):
                b_cp(d, k).start()

            @pl.when(d > 0)
            def _():
                b_cp(d, 0).start()

            @pl.when(d == 0)
            def _():
                own_cp().start()

    for j in range(4):
        core_cp[j].wait_send()
    for j in range(2):
        rel_cp[j].wait_send()
        fin_cp[j].wait_send()
        z_half[j].wait_send()
    for cp in u_cp:
        cp.wait_send()
    for d in (1, 2, 3, 5, 6, 7):
        z_in(d).wait_send()

    @pl.loop(0, 8)
    def _(d):
        for k in range(4):
            y_cp(d, k).wait_send()
            c_cp(d, k).wait_send()
        for k in range(1, NX):
            x_cp(d, k).wait_send()
            b_cp(d, k).wait_send()
            b_cp(d, k).wait_recv()

    own_cp().wait()

    @pl.loop(1, 8)
    def _(d):
        b_cp(d, 0).wait_send()
        b_cp(d, 0).wait_recv()


def pick_kernel(rel_rows, rel_flat, ret, out):
    rel = rel_rows[...].astype(F32)
    group = iota((32, 64), 0).astype(F32)
    hit = jnp.zeros((32, 64), F32)
    for k in range(4):
        hit = hit + jnp.where(rel[k:k + 1, :] == group, 1.0, 0.0)
    tri = jnp.where(iota((64, 256), 0) < iota((64, 256), 1) % 64, 1.0, 0.0).astype(BF16)
    rank = jnp.dot(hit.astype(BF16), tri, preferred_element_type=F32)
    flat = rel_flat[...].astype(F32)
    mine = jnp.where(flat == iota((32, 256), 0).astype(F32), rank, 0.0)
    slot = jnp.sum(mine, axis=0, keepdims=True)
    key = jnp.where(slot < 15.5, flat * 16.0 + slot, -1.0)
    key0 = jnp.where(slot > 15.5, flat * 8.0 + slot - 16.0, -1.0)
    key1 = jnp.where(slot > 15.5, flat * 8.0 + slot - 12.0, -1.0)
    hot = jnp.where(iota((512, 256), 0).astype(F32) == key, 1.0, 0.0).astype(BF16)
    hot0 = jnp.where(iota((256, 256), 0).astype(F32) == key0, 1.0, 0.0).astype(BF16)
    hot1 = jnp.where(iota((256, 256), 0).astype(F32) == key1, 1.0, 0.0).astype(BF16)
    TN = (((0,), (0,)), ((), ()))
    for j in range(5):
        main = ret[:, :, 16 * j:16 * j + 16, :].reshape(512, 128)
        i = j % 3
        more = ret[:, :, 80 + 8 * i:88 + 8 * i, :].reshape(256, 128)
        res = lax.dot_general(hot, main, TN, preferred_element_type=F32) + lax.dot_general(
            hot0 if j < 3 else hot1, more, TN, preferred_element_type=F32
        )
        for k in range(4):
            out[:, k, 128 * j:128 * j + 128] = res[64 * k:64 * k + 64]


def local(activations, out_grads, proj_in, proj_out, queries, candidates):
    dp = lax.axis_index("dp")
    cand_t = jnp.pad(candidates.T, ((0, 4), (0, 0)), constant_values=-1)
    rel = (cand_t % NZ - dp % NZ + NZ) % NZ * NX + (cand_t // NZ - dp // NZ + NX) % NX
    vm = pl.BlockSpec(memory_space=pltpu.VMEM)
    hbm = pl.BlockSpec(memory_space=pl.ANY)
    dma = pltpu.SemaphoreType.DMA
    ret = pl.pallas_call(
        main_kernel,
        name="attribution",
        out_shape=jax.ShapeDtypeStruct((8, 4, 104, 128), BF16),
        in_specs=[hbm, hbm, vm, vm, hbm, vm],
        out_specs=vm,
        scratch_shapes=[
            pltpu.VMEM((8, 192, 1792), BF16),
            pltpu.VMEM((8, 192, 512), BF16),
            pltpu.VMEM((128, 1792), BF16),
            pltpu.VMEM((128, 512), BF16),
            pltpu.VMEM((256, 4096), BF16),
            pltpu.VMEM((8, 192, 128), F32),
            pltpu.VMEM((4, 192, 128), F32),
            pltpu.VMEM((192, 128), F32),
            pltpu.VMEM((2, 96, 128), F32),
            pltpu.VMEM((2, 192, 128), F32),
            pltpu.VMEM((2, 192, 128), F32),
            pltpu.VMEM((192, 128), F32),
            pltpu.VMEM((8, 4096), F32),
            pltpu.VMEM((8, 16, 256), BF16),
            pltpu.VMEM((8, 136, 256), BF16),
            pltpu.VMEM((8, 4, 40, 256), BF16),
            pltpu.VMEM((8, 8, 4, 40, 256), BF16),
            pltpu.VMEM((640, 2048), BF16),
            pltpu.VMEM((640, 2048), BF16),
            pltpu.VMEM((8, 4, 104, 128), BF16),
            dma((8,)), dma((8,)), dma((16,)),
            dma((4,)), dma((4,)), dma((2,)), dma((2,)), dma((2,)), dma((2,)), dma((8,)), dma((8,)),
            dma((8,)), dma((8,)), dma((8, 4)), dma((8, 4)), dma((8, 4)), dma((8, 4)),
            dma((8, 4)), dma((8, 4)), dma((8, 4)), dma((8, 4)),
        ],
        compiler_params=pltpu.CompilerParams(
            collective_id=0, has_side_effects=True, vmem_limit_bytes=56 * 1024 * 1024
        ),
    )(
        activations.reshape(1536, 1792), out_grads.reshape(1536, 512),
        proj_in.T, proj_out.T, queries[0], cand_t,
    )
    return pl.pallas_call(
        pick_kernel,
        name="pick",
        out_shape=jax.ShapeDtypeStruct((64, 4, 640), F32),
        in_specs=[vm, vm, vm],
        out_specs=vm,
    )(rel, rel[0:4].reshape(1, 256), ret)


def solution(mesh):
    placed = (
        P("dp", None, "tensor"),
        P("dp", None, "tensor"),
        P("tensor", None),
        P("tensor", None),
        P("dp", "tensor", None),
        P("dp", None),
    )
    return jax.shard_map(
        local, mesh=mesh, in_specs=placed, out_specs=P("dp", None, "tensor"), check_vma=False
    )
```

```python
import jax
import jax.numpy as jnp
from jax import lax
from jax.experimental import pallas as pl
from jax.experimental.pallas import tpu as pltpu
from jax.sharding import PartitionSpec as P

EPS = 1e-06
NX, NZ, NY = 4, 8, 4
F32, BF16, I32 = jnp.float32, jnp.bfloat16, jnp.int32
NT = (((1,), (1,)), ((), ()))


def iota(shape, axis):
    return lax.broadcasted_iota(I32, shape, axis)


def main_kernel(
    act, og, pin, pout, qh, cand, ret,
    abuf, obuf, wa, wo, expand, part, rcore, csum, rrel, fin, rfin, pbuf, ubuf32, usend,
    zb, cb, hotb, xs, r, q0, q1, rs, tbuf,
    act_sem, og_sem, q_sem,
    cb_s, cb_r, core_s, core_r, rel_s, rel_r, fin_s, fin_r, u_s, u_r,
    z_s, z_r, x_s, x_r, y_s, y_r, c_s, c_r, b_s, b_r, t_s, t_r,
):
    dp = lax.axis_index("dp")
    t = lax.axis_index("tensor")
    x, z = dp // NZ, dp % NZ
    y, c = t // 2, t % 2

    def dev(dp_to, t_to):
        return {"dp": dp_to, "tensor": t_to}

    def rcopy(src, dst, ss, rr, to):
        return pltpu.make_async_remote_copy(
            src_ref=src, dst_ref=dst, send_sem=ss, recv_sem=rr,
            device_id=to, device_id_type=pl.DeviceIdType.MESH,
        )

    partner = dev(dp, 2 * y + (1 - c))
    yup = dev(dp, 2 * ((y + 1) % NY) + c)
    ydn = dev(dp, 2 * ((y + NY - 1) % NY) + c)
    zup = dev(x * NZ + (z + 1) % NZ, t)
    zdn = dev(x * NZ + (z + NZ - 1) % NZ, t)

    barrier = pltpu.get_barrier_semaphore()

    def greet(to):
        pl.semaphore_signal(barrier, inc=1, device_id=to, device_id_type=pl.DeviceIdType.MESH)

    for k in range(1, 8):
        greet(dev(dp, (t + k) % 8))
    for d in (1, 2, 6, 7):
        for k in range(8):
            greet(dev(x * NZ + (z + d) % NZ, (t + k) % 8))
    for d in (3, 4, 5):
        greet(dev(x * NZ + (z + d) % NZ, t))
    for k in range(1, NX):
        greet(dev((x + k) % NX * NZ + z, t))

    ys = [(y + 2) % NY, (y + 1) % NY, (y + 3) % NY, y]
    for n in range(8):
        tb = 2 * ys[n // 2] + ((1 - c) if n % 2 == 0 else c)
        rows = pl.ds(pl.multiple_of(tb * 192, 192), 192)
        a = pltpu.make_async_copy(act.at[rows, :], abuf.at[n // 2, pl.ds(n % 2 * 192, 192)], act_sem.at[n // 2])
        o = pltpu.make_async_copy(og.at[rows, :], obuf.at[n // 2, pl.ds(n % 2 * 192, 192)], og_sem.at[n // 2])
        a.start()
        o.start()

    wa[0:64, :] = jnp.zeros((64, wa.shape[1]), BF16)
    wa[64:128, :] = pin[...]
    wo[0:64, :] = pout[...]
    wo[64:128, :] = jnp.zeros((64, wo.shape[1]), BF16)

    def project(j):
        pltpu.make_async_copy(act.at[pl.ds(0, 384), :], abuf.at[j], act_sem.at[j]).wait()
        pltpu.make_async_copy(og.at[pl.ds(0, 384), :], obuf.at[j], og_sem.at[j]).wait()
        both = lax.dot_general(
            abuf[j], wa[...], NT, preferred_element_type=F32
        ) + lax.dot_general(obuf[j], wo[...], NT, preferred_element_type=F32)
        part[2 * j] = both[0:192]
        part[2 * j + 1] = both[192:384]

    core_cp = [rcopy(part.at[2 * j], rcore.at[j], core_s.at[j], core_r.at[j], partner)
               for j in range(4)]
    rel_cp = [rcopy(csum.at[pl.ds(0, 96)], rrel.at[0], rel_s.at[0], rel_r.at[0], yup),
              rcopy(csum.at[pl.ds(96, 96)], rrel.at[1], rel_s.at[1], rel_r.at[1], ydn)]
    top, low_half = pl.ds(0, 96), pl.ds(96, 96)

    def fin_copy(j, early):
        rows = (low_half if early else top) if j == 0 else (top if early else low_half)
        n = 2 * j + (0 if early else 1)
        return rcopy(fin.at[j, rows], rfin.at[j, rows], fin_s.at[n], fin_r.at[n],
                     yup if j == 0 else ydn)

    fin_cp = [fin_copy(j, early) for j in (0, 1) for early in (True, False)]

    e_of = iota((64, 128), 1) // 16 * 8 + iota((64, 128), 1) % 8
    dup = jnp.where(iota((64, 128), 0) == e_of, 1.0, 0.0).astype(BF16)
    c2 = jnp.dot(cand[...].astype(F32).astype(BF16), dup, preferred_element_type=F32)
    cb[0] = jnp.concatenate([c2, jnp.full((4, 128), -1.0, F32)], axis=0).astype(BF16)

    def cand_cp(d):
        return rcopy(cb.at[0], cb.at[d], cb_s.at[0], cb_r.at[0], dev(x * NZ + (z + d) % NZ, t))

    project(0)
    pl.semaphore_wait(barrier, 7 + 32 + 3 + NX - 1)
    core_cp[0].start()
    for d in range(1, 8):
        cand_cp(d).start()
    project(1)
    core_cp[1].start()
    core_cp[0].wait_recv()
    csum[...] = part[1] + rcore[0]
    rel_cp[0].start()
    rel_cp[1].start()
    core_cp[1].wait_recv()
    fin[0, 96:192] = part[3, 96:192] + rcore[1, 96:192]
    fin_cp[0].start()
    project(2)
    core_cp[2].start()
    project(3)
    core_cp[3].start()
    core_cp[2].wait_recv()
    fin[1, 0:96] = part[5, 0:96] + rcore[2, 0:96]
    fin_cp[2].start()

    rel_y = [y, (y + 3) % NY, (y + 1) % NY, (y + 2) % NY]
    for rel in range(8):
        ts = 2 * rel_y[rel // 2] + (c if rel % 2 == 0 else 1 - c)
        for h, dst in ((0, q0), (1, q1)):
            cols = pl.ds(pl.multiple_of(ts * 512 + h * 256, 256), 256)
            cp = pltpu.make_async_copy(
                qh.at[:, cols], dst.at[:, pl.ds(rel * 256, 256)], q_sem.at[h]
            )
            cp.start()

    row = iota((256, 4096), 0)
    col = iota((256, 4096), 1)
    expand[...] = jnp.where((row % 64 == col // 64) & (row < 192), 1.0, 0.0).astype(BF16)
    rel_cp[0].wait_recv()
    fin[0, 0:96] = part[3, 0:96] + rcore[1, 0:96] + rrel[0]
    fin_cp[1].start()
    rel_cp[1].wait_recv()
    fin[1, 96:192] = part[5, 96:192] + rcore[2, 96:192] + rrel[1]
    fin_cp[3].start()
    tri_r, tri_c = iota((128, 128), 0), iota((128, 128), 1)
    tri = jnp.where(
        ((tri_r // 8) % 2 == 0)
        & (tri_r // 16 * 8 + tri_r % 8 < tri_c // 16 * 8 + tri_c % 8), 1.0, 0.0
    ).astype(BF16)
    mr = iota((40, 128), 0)
    slot_of = jnp.where(mr < 16, mr, jnp.where(mr < 20, mr, jnp.where(mr < 24, mr - 4, mr - 24)))
    half_of = jnp.where(mr < 20, 0, 1)
    rowkey = (slot_of + 64 * half_of).astype(F32)
    half_lane = ((iota((1, 128), 1) // 8) % 2 * 64).astype(F32)

    def choose(d):
        cz = cb[d].astype(F32)
        eqs = []
        for k in range(NX):
            g = ((x + k) % NX * NZ + z).astype(F32)
            eqs.append(jnp.where(cz == g, 1.0, 0.0))
        ranks = jnp.dot(jnp.concatenate(eqs, axis=0).astype(BF16), tri,
                        preferred_element_type=F32)
        for k in range(NX):
            hit = jnp.sum(eqs[k], axis=0, keepdims=True)
            rank = jnp.sum(ranks[8 * k:8 * k + 8], axis=0, keepdims=True)
            key = jnp.where(hit > 0.5, rank + half_lane, -1.0)
            hotb[d, 40 * k:40 * k + 40, :] = jnp.where(rowkey == key, 1.0, 0.0).astype(BF16)

    cand_all = rcopy(cb.at[pl.ds(1, 7)], cb.at[pl.ds(1, 7)], cb_s.at[0], cb_r.at[0], zup)
    cand_all.wait_recv()
    for d in range(8):
        choose(d)
    core_cp[3].wait_recv()
    for cp in fin_cp:
        cp.wait_recv()
    pbuf[...] = part[7] + rcore[3] + rfin[0] + rfin[1]

    pt = jnp.concatenate([pbuf[pl.ds(k, 8, stride=24), :] for k in range(24)], axis=0)
    lane = iota((192, 128), 1)
    low = lane < 64
    a2 = jnp.where(low, pltpu.roll(pt, 64, 1), pt)
    a4 = jnp.concatenate([a2, a2], axis=1)
    hi = pt.astype(BF16).astype(F32)
    rest = pt - hi
    mid = rest.astype(BF16).astype(F32)
    lo = rest - mid
    g3 = jnp.concatenate(
        [jnp.where(low, hi, pltpu.roll(mid, 64, 1)), jnp.where(low, lo, 0.0)], axis=1
    ).astype(BF16)
    sq = jnp.zeros((8, 256), F32)
    for m in range(16):
        gx = jnp.dot(g3, expand[:, 256 * m:256 * m + 256], preferred_element_type=F32)
        u = jnp.sum((gx * a4).reshape(24, 8, 256), axis=0)
        ubuf32[:, 256 * m:256 * m + 256] = u
        sq = sq + u * u
    inv = lax.rsqrt(jnp.sum(sq, axis=1, keepdims=True) / 4096.0 + EPS)
    for m in range(16):
        usend[m // 2, 8 * (m % 2):8 * (m % 2) + 8, :] = (
            ubuf32[:, 256 * m:256 * m + 256] * inv
        ).astype(BF16)
    my_rows = pl.ds(pl.multiple_of(t * 16, 16), 16)
    zb[0, my_rows, :] = usend[t]

    def u_cp(d, k):
        to = (t + k) % 8
        return rcopy(usend.at[to], zb.at[d, my_rows, :], u_s.at[d], u_r.at[d],
                     dev(x * NZ + (z + d) % NZ, to))

    near = (0, 1, 7, 2, 6)
    for d in near:
        for k in range(8):
            if (d, k) != (0, 0):
                u_cp(d, k).start()

    def u_all(d):
        n = 7 if d == 0 else 8
        return rcopy(zb.at[d, pl.ds(0, 16 * n)], zb.at[d, pl.ds(0, 16 * n)], u_s.at[d], u_r.at[d], zup)

    def z_in(d):
        return rcopy(zb.at[d], zb.at[d], z_s.at[d], z_r.at[d], zup)

    z_half = [rcopy(zb.at[3, pl.ds(0, 64)], zb.at[4, pl.ds(0, 64)], z_s.at[4], z_r.at[4], zup),
              rcopy(zb.at[5, pl.ds(64, 64)], zb.at[4, pl.ds(64, 64)], z_s.at[0], z_r.at[0], zdn)]
    z_far = [rcopy(zb.at[2], zb.at[3], z_s.at[3], z_r.at[3], zup),
             rcopy(zb.at[6], zb.at[5], z_s.at[5], z_r.at[5], zdn)]

    def x_cp(d, k):
        return rcopy(xs.at[d, k], r.at[0, d, k], x_s.at[0], x_r.at[d],
                     dev((x + k) % NX * NZ + z, t))

    def y_cp(d, k):
        if k == 0:
            return rcopy(r.at[0, d], r.at[2, d], y_s.at[0], y_r.at[0, d], yup)
        if k == 1:
            return rcopy(r.at[0, d], r.at[4, d], y_s.at[1], y_r.at[0, d], ydn)
        if k == 2:
            return rcopy(r.at[2, d, pl.ds(0, 2)], r.at[6, d, pl.ds(0, 2)],
                         y_s.at[2], y_r.at[1, d], yup)
        return rcopy(r.at[4, d, pl.ds(2, 2)], r.at[6, d, pl.ds(2, 2)],
                     y_s.at[2], y_r.at[1, d], ydn)

    def c_cp(d, k):
        return rcopy(r.at[2 * k, d], r.at[2 * k + 1, d], c_s.at[k], c_r.at[d], partner)

    def b_cp(d, k):
        to = (x + NX - k) % NX * NZ + (z + NZ - d) % NZ
        return rcopy(rs.at[d, k], ret.at[d, k], b_s.at[1 if d == 0 else 0], b_r.at[d], dev(to, t))

    def t_cp(k):
        to = x * NZ + (z + (2 if k < 2 else NZ - 2)) % NZ
        return rcopy(rs.at[4, k], tbuf.at[k], b_s.at[0], t_r.at[k], dev(to, t))

    def t_on(k):
        to = (x + NX - k) % NX * NZ + (z + (2 if k < 2 else NZ - 2)) % NZ
        return rcopy(tbuf.at[k], ret.at[4, k], t_s.at[0], b_r.at[4], dev(to, t))

    def own_cp():
        return pltpu.make_async_copy(rs.at[0, 0], ret.at[0, 0], b_s.at[2])

    def pack(d):
        msg = jnp.dot(hotb[d], zb[d], preferred_element_type=F32)
        r[0, d, 0] = msg[0:40].astype(BF16)
        for k in range(1, NX):
            xs[d, k] = msg[40 * k:40 * k + 40].astype(BF16)

    row8 = iota((8, 128), 0)

    def scores(d):
        l0 = jnp.concatenate([r[k, d, :, 0:24, :].reshape(96, 256) for k in range(8)], axis=1)
        l1 = jnp.concatenate([r[k, d, :, 16:40, :].reshape(96, 256) for k in range(8)], axis=1)
        acc0 = lax.dot_general(l0, q0[...], NT, preferred_element_type=F32)
        acc1 = lax.dot_general(l1, q1[...], NT, preferred_element_type=F32)
        for k in range(NX):
            b = 24 * k
            m = acc0[b:b + 16] + acc1[b + 8:b + 24]
            ex = acc0[b + 16:b + 24] + pltpu.roll(acc1[b:b + 8], 4, 0)
            ex2 = pltpu.roll(ex, 4, 0)
            for j in range(5):
                rs[d, k, 16 * j:16 * j + 16, :] = m[:, 128 * j:128 * j + 128].astype(BF16)
            for j in range(3):
                v = ex[:, 128 * j:128 * j + 128]
                if j < 2:
                    v = jnp.where(row8 < 4, v, ex2[:, 128 * j + 384:128 * j + 512])
                rs[d, k, 80 + 8 * j:88 + 8 * j, :] = v.astype(BF16)

    def s1(d):
        pack(d)
        for k in range(1, NX):
            x_cp(d, k).start()

    def s2(d):
        rcopy(r.at[0, d, pl.ds(1, 3)], r.at[0, d, pl.ds(1, 3)], x_s.at[0], x_r.at[d], zup).wait_recv()
        y_cp(d, 0).start()
        y_cp(d, 1).start()
        c_cp(d, 0).start()

    def s3(d):
        rcopy(r.at[pl.ds(0, 2), d], r.at[pl.ds(0, 2), d], y_s.at[0], y_r.at[0, d], zup).wait_recv()
        y_cp(d, 2).start()
        y_cp(d, 3).start()
        c_cp(d, 1).start()
        c_cp(d, 2).start()

    def s4(d):
        rcopy(r.at[6, d], r.at[6, d], y_s.at[2], y_r.at[1, d], zup).wait_recv()
        c_cp(d, 3).start()

    def s5(d):
        rcopy(r.at[pl.ds(0, 4), d], r.at[pl.ds(0, 4), d], c_s.at[0], c_r.at[d], zup).wait_recv()
        scores(d)
        for k in range(NX):
            if d == 4:
                t_cp(k).start()
            elif (d, k) == (0, 0):
                own_cp().start()
            else:
                b_cp(d, k).start()

    def u_wait(d):
        u_all(d).wait_recv()

    for d in near:
        u_wait(d)
        if d == 2:
            z_far[0].start()
        if d == 6:
            z_far[1].start()
        s1(d)
    for h, dst in ((0, q0), (1, q1)):
        pltpu.make_async_copy(qh.at[:, pl.ds(0, 2048)], dst, q_sem.at[h]).wait()
    s2(1)
    z_far[0].wait_recv()
    z_half[0].start()
    s1(3)
    z_far[1].wait_recv()
    z_half[1].start()
    s1(5)
    s2(6), s3(1), s2(3)
    z_half[0].wait_recv()
    z_half[1].wait_recv()
    s1(4)
    s3(6), s2(5)
    s4(1), s3(3), s5(1), s2(4)
    s4(6), s3(5), s2(2), s5(6)
    s4(3), s3(4), s2(7), s5(3)
    s4(5), s3(2), s2(0), s4(4), s5(5)
    s3(7), s4(2), s5(4)
    s3(0), s4(7), s5(2)
    s4(0), s5(7)

    def relay(ks):
        for k in ks:
            t_cp(k).wait_recv()
            t_on(k).start()

    relay((2, 3))
    s5(0)
    relay((0, 1))

    def sent():
        for j in range(4):
            core_cp[j].wait_send()
            fin_cp[j].wait_send()
        for j in range(2):
            rel_cp[j].wait_send()
            z_half[j].wait_send()
        for d in near:
            u_all(d).wait_send()
        cand_all.wait_send()
        for cp in z_far:
            cp.wait_send()

        rcopy(xs.at[:, pl.ds(1, 3)], xs.at[:, pl.ds(1, 3)], x_s.at[0], x_r.at[0], zup).wait_send()
        for k in range(3):
            rcopy(r.at[k], r.at[k], y_s.at[k], y_r.at[0, 0], zup).wait_send()
        for k in range(4):
            rcopy(r.at[k], r.at[k], c_s.at[k], c_r.at[0], zup).wait_send()

    sent()

    def got(d):
        if d == 0:
            own_cp().wait()
            some = ret.at[0, pl.ds(1, 3)]
        else:
            some = ret.at[d]
        rcopy(some, some, b_s.at[0], b_r.at[d], zup).wait_recv()

    for d in (1, 6, 3, 5, 2, 7, 0, 4):
        got(d)

    def returned():
        some = rs.at[pl.ds(1, 7)]
        rcopy(some, some, b_s.at[0], b_r.at[1], zup).wait_send()
        some = rs.at[0, pl.ds(1, 3)]
        rcopy(some, some, b_s.at[1], b_r.at[0], zup).wait_send()
        rcopy(tbuf, tbuf, t_s.at[0], t_r.at[0], zup).wait_send()

    returned()


def pick_kernel(cand, ret, out):
    dp = lax.axis_index("dp")
    cd = cand[...]
    rel = ((cd % NZ - dp % NZ + NZ) % NZ * NX + (cd // NZ - dp // NZ + NX) % NX).astype(F32)
    group = iota((32, 64), 0).astype(F32)
    hit = jnp.zeros((32, 64), F32)
    for k in range(4):
        hit = hit + jnp.where(rel[k:k + 1, :] == group, 1.0, 0.0)
    tri = jnp.where(iota((64, 256), 0) < iota((64, 256), 1) % 64, 1.0, 0.0).astype(BF16)
    rank = jnp.dot(hit.astype(BF16), tri, preferred_element_type=F32)
    lane = iota((64, 256), 1)
    dup = jnp.where(iota((64, 256), 0) == lane % 64, 1.0, 0.0).astype(BF16)
    wide = jnp.dot(rel.astype(BF16), dup, preferred_element_type=F32)
    flat = jnp.sum(jnp.where(iota((4, 256), 0) == iota((4, 256), 1) // 64, wide, 0.0),
                   axis=0, keepdims=True)
    mine = jnp.where(flat == iota((32, 256), 0).astype(F32), rank, 0.0)
    slot = jnp.sum(mine, axis=0, keepdims=True)
    rows = jnp.concatenate([flat, slot, jnp.zeros((6, 256), F32)], axis=0).astype(BF16)
    eye = jnp.where(iota((8, 128), 0) == iota((8, 128), 1), 1.0, 0.0).astype(BF16)
    cols = lax.dot_general(rows, eye, (((0,), (0,)), ((), ())), preferred_element_type=F32)
    relc, slotc = cols[:, 0:1], cols[:, 1:2]
    key = jnp.where(slotc < 15.5, relc * 16.0 + slotc, -1.0)
    key0 = jnp.where(slotc > 15.5, relc * 8.0 + slotc - 16.0, -1.0)
    key1 = jnp.where(slotc > 15.5, relc * 8.0 + slotc - 12.0, -1.0)
    at512 = iota((256, 512), 1).astype(F32)
    at256 = iota((256, 256), 1).astype(F32)
    hot = jnp.where(at512 == key, 1.0, 0.0).astype(BF16)
    hot0 = jnp.where(at256 == key0, 1.0, 0.0).astype(BF16)
    hot1 = jnp.where(at256 == key1, 1.0, 0.0).astype(BF16)
    for js, more in (((0, 1, 2), hot0), ((3, 4), hot1)):
        pick = jnp.concatenate([hot, more], axis=1)
        vals = jnp.concatenate(
            [jnp.concatenate([
                ret[:, :, 16 * j:16 * j + 16, :].reshape(512, 128),
                ret[:, :, 80 + 8 * (j % 3):88 + 8 * (j % 3), :].reshape(256, 128),
            ], axis=0) for j in js], axis=1)
        res = jnp.dot(pick, vals, preferred_element_type=F32)
        for k in range(4):
            out[:, k, 128 * js[0]:128 * js[-1] + 128] = res[64 * k:64 * k + 64]


def local(activations, out_grads, proj_in, proj_out, queries, candidates):
    cand_t = candidates.T
    vm = pl.BlockSpec(memory_space=pltpu.VMEM)
    hbm = pl.BlockSpec(memory_space=pl.ANY)
    dma = pltpu.SemaphoreType.DMA
    ret = pl.pallas_call(
        main_kernel,
        name="attribution",
        out_shape=jax.ShapeDtypeStruct((8, 4, 104, 128), BF16),
        in_specs=[hbm, hbm, vm, vm, hbm, vm],
        out_specs=hbm,
        scratch_shapes=[
            pltpu.VMEM((4, 384, 1792), BF16),
            pltpu.VMEM((4, 384, 512), BF16),
            pltpu.VMEM((128, 1792), BF16),
            pltpu.VMEM((128, 512), BF16),
            pltpu.VMEM((256, 4096), BF16),
            pltpu.VMEM((8, 192, 128), F32),
            pltpu.VMEM((4, 192, 128), F32),
            pltpu.VMEM((192, 128), F32),
            pltpu.VMEM((2, 96, 128), F32),
            pltpu.VMEM((2, 192, 128), F32),
            pltpu.VMEM((2, 192, 128), F32),
            pltpu.VMEM((192, 128), F32),
            pltpu.VMEM((8, 4096), F32),
            pltpu.VMEM((8, 16, 256), BF16),
            pltpu.VMEM((8, 128, 256), BF16),
            pltpu.VMEM((8, 8, 128), BF16),
            pltpu.VMEM((8, 160, 128), BF16),
            pltpu.VMEM((8, 4, 40, 256), BF16),
            pltpu.VMEM((8, 8, 4, 40, 256), BF16),
            pltpu.VMEM((640, 2048), BF16),
            pltpu.VMEM((640, 2048), BF16),
            pltpu.VMEM((8, 4, 104, 128), BF16),
            pltpu.VMEM((4, 104, 128), BF16),
            dma((4,)), dma((4,)), dma((2,)),
            dma((1,)), dma((1,)), dma((4,)), dma((4,)), dma((2,)), dma((2,)), dma((4,)), dma((4,)),
            dma((8,)), dma((8,)), dma((8,)), dma((8,)), dma((1,)), dma((8,)), dma((3,)), dma((2, 8)),
            dma((4,)), dma((8,)), dma((3,)), dma((8,)), dma((1,)), dma((4,)),
        ],
        compiler_params=pltpu.CompilerParams(
            collective_id=0, has_side_effects=True, vmem_limit_bytes=56 * 1024 * 1024
        ),
    )(
        activations.reshape(1536, 1792), out_grads.reshape(1536, 512),
        proj_in.T, proj_out.T, queries[0], cand_t,
    )
    return pl.pallas_call(
        pick_kernel,
        name="pick",
        out_shape=jax.ShapeDtypeStruct((64, 4, 640), F32),
        in_specs=[vm, vm],
        out_specs=vm,
    )(cand_t, ret)


def solution(mesh):
    placed = (
        P("dp", None, "tensor"),
        P("dp", None, "tensor"),
        P("tensor", None),
        P("tensor", None),
        P("dp", "tensor", None),
        P("dp", None),
    )
    return jax.shard_map(
        local, mesh=mesh, in_specs=placed, out_specs=P("dp", None, "tensor"), check_vma=False
    )
```

```python
import jax
import jax.numpy as jnp
from jax import lax
from jax.experimental import pallas as pl
from jax.experimental.pallas import tpu as pltpu
from jax.sharding import PartitionSpec as P

EPS = 1e-06
NX, NZ, NY = 4, 8, 4
F32, BF16, I32 = jnp.float32, jnp.bfloat16, jnp.int32
NT = (((1,), (1,)), ((), ()))


def iota(shape, axis):
    return lax.broadcasted_iota(I32, shape, axis)


def main_kernel(
    act, og, pin, pout, qh, cand, ret,
    abuf, obuf, wa, wo, expand, part, rcore, csum, rrel, fin, rfin, pbuf, ubuf32, usend,
    zb, cb, hotb, xs, r, q0, q1, rs, tbuf,
    cbuf, act_sem, og_sem, q_sem, w_sem,
    cb_s, cb_r, core_s, core_r, rel_s, rel_r, fin_s, fin_r, u_s, u_r,
    z_s, z_r, x_s, x_r, y_s, y_r, c_s, c_r, b_s, b_r, t_s, t_r,
):
    dp = lax.axis_index("dp")
    t = lax.axis_index("tensor")
    x, z = dp // NZ, dp % NZ
    y, c = t // 2, t % 2

    def dev(dp_to, t_to):
        return {"dp": dp_to, "tensor": t_to}

    def rcopy(src, dst, ss, rr, to):
        return pltpu.make_async_remote_copy(
            src_ref=src, dst_ref=dst, send_sem=ss, recv_sem=rr,
            device_id=to, device_id_type=pl.DeviceIdType.MESH,
        )

    partner = dev(dp, 2 * y + (1 - c))
    yup = dev(dp, 2 * ((y + 1) % NY) + c)
    ydn = dev(dp, 2 * ((y + NY - 1) % NY) + c)
    zup = dev(x * NZ + (z + 1) % NZ, t)
    zdn = dev(x * NZ + (z + NZ - 1) % NZ, t)

    barrier = pltpu.get_barrier_semaphore()

    def greet(to):
        pl.semaphore_signal(barrier, inc=1, device_id=to, device_id_type=pl.DeviceIdType.MESH)

    for k in range(1, 8):
        greet(dev(dp, (t + k) % 8))
    for d in (1, 2, 6, 7):
        for k in range(8):
            greet(dev(x * NZ + (z + d) % NZ, (t + k) % 8))
    for d in (3, 4, 5):
        greet(dev(x * NZ + (z + d) % NZ, t))
    for k in range(1, NX):
        greet(dev((x + k) % NX * NZ + z, t))

    ys = [(y + 2) % NY, (y + 1) % NY, (y + 3) % NY, y]

    def load(j):
        for n in (2 * j, 2 * j + 1):
            tb = 2 * ys[j] + ((1 - c) if n % 2 == 0 else c)
            rows = pl.ds(pl.multiple_of(tb * 192, 192), 192)
            part_rows = pl.ds(n % 2 * 192, 192)
            pltpu.make_async_copy(act.at[rows, :], abuf.at[j, part_rows], act_sem.at[j]).start()
            pltpu.make_async_copy(og.at[rows, :], obuf.at[j, part_rows], og_sem.at[j]).start()

    small = [
        pltpu.make_async_copy(pin, wa.at[pl.ds(64, 64)], w_sem.at[0]),
        pltpu.make_async_copy(pout, wo.at[pl.ds(0, 64)], w_sem.at[1]),
        pltpu.make_async_copy(cand, cbuf, w_sem.at[2]),
    ]
    for cp in small:
        cp.start()
    load(0)
    load(1)

    wa[0:64, :] = jnp.zeros((64, wa.shape[1]), BF16)
    wo[64:128, :] = jnp.zeros((64, wo.shape[1]), BF16)
    small[0].wait()
    small[1].wait()

    def project(j):
        pltpu.make_async_copy(act.at[pl.ds(0, 384), :], abuf.at[j], act_sem.at[j]).wait()
        pltpu.make_async_copy(og.at[pl.ds(0, 384), :], obuf.at[j], og_sem.at[j]).wait()
        if j < 2:
            load(j + 2)
        both = lax.dot_general(
            abuf[j], wa[...], NT, preferred_element_type=F32
        ) + lax.dot_general(obuf[j], wo[...], NT, preferred_element_type=F32)
        part[2 * j] = both[0:192]
        part[2 * j + 1] = both[192:384]

    core_cp = [rcopy(part.at[2 * j], rcore.at[j], core_s.at[j], core_r.at[j], partner)
               for j in range(4)]
    rel_cp = [rcopy(csum.at[pl.ds(0, 96)], rrel.at[0], rel_s.at[0], rel_r.at[0], yup),
              rcopy(csum.at[pl.ds(96, 96)], rrel.at[1], rel_s.at[1], rel_r.at[1], ydn)]
    top, low_half = pl.ds(0, 96), pl.ds(96, 96)

    def fin_copy(j, early):
        rows = (low_half if early else top) if j == 0 else (top if early else low_half)
        n = 2 * j + (0 if early else 1)
        return rcopy(fin.at[j, rows], rfin.at[j, rows], fin_s.at[n], fin_r.at[n],
                     yup if j == 0 else ydn)

    fin_cp = [fin_copy(j, early) for j in (0, 1) for early in (True, False)]

    def cand_cp(d):
        return rcopy(cb.at[0], cb.at[d], cb_s.at[0], cb_r.at[0], dev(x * NZ + (z + d) % NZ, t))

    project(0)
    pl.semaphore_wait(barrier, 7 + 32 + 3 + NX - 1)
    core_cp[0].start()
    project(1)
    core_cp[1].start()
    core_cp[0].wait_recv()
    csum[...] = part[1] + rcore[0]
    rel_cp[0].start()
    rel_cp[1].start()
    small[2].wait()
    e_of = iota((64, 128), 1) // 16 * 8 + iota((64, 128), 1) % 8
    dup = jnp.where(iota((64, 128), 0) == e_of, 1.0, 0.0).astype(BF16)
    c2 = jnp.dot(cbuf[...].astype(F32).astype(BF16), dup, preferred_element_type=F32)
    cb[0] = jnp.concatenate([c2, jnp.full((4, 128), -1.0, F32)], axis=0).astype(BF16)

    for d in range(1, 8):
        cand_cp(d).start()
    project(2)
    core_cp[2].start()
    core_cp[1].wait_recv()
    fin[0, 96:192] = part[3, 96:192] + rcore[1, 96:192]
    fin_cp[0].start()
    project(3)
    core_cp[3].start()
    core_cp[2].wait_recv()
    fin[1, 0:96] = part[5, 0:96] + rcore[2, 0:96]
    fin_cp[2].start()

    rel_y = [y, (y + 3) % NY, (y + 1) % NY, (y + 2) % NY]
    for rel in range(8):
        ts = 2 * rel_y[rel // 2] + (c if rel % 2 == 0 else 1 - c)
        for h, dst in ((0, q0), (1, q1)):
            cols = pl.ds(pl.multiple_of(ts * 512 + h * 256, 256), 256)
            cp = pltpu.make_async_copy(
                qh.at[:, cols], dst.at[:, pl.ds(rel * 256, 256)], q_sem.at[h]
            )
            cp.start()

    row = iota((256, 4096), 0)
    col = iota((256, 4096), 1)
    expand[...] = jnp.where((row % 64 == col // 64) & (row < 192), 1.0, 0.0).astype(BF16)
    rel_cp[0].wait_recv()
    fin[0, 0:96] = part[3, 0:96] + rcore[1, 0:96] + rrel[0]
    fin_cp[1].start()
    rel_cp[1].wait_recv()
    fin[1, 96:192] = part[5, 96:192] + rcore[2, 96:192] + rrel[1]
    fin_cp[3].start()
    tri_r, tri_c = iota((128, 128), 0), iota((128, 128), 1)
    tri = jnp.where(
        ((tri_r // 8) % 2 == 0)
        & (tri_r // 16 * 8 + tri_r % 8 < tri_c // 16 * 8 + tri_c % 8), 1.0, 0.0
    ).astype(BF16)
    mr = iota((40, 128), 0)
    slot_of = jnp.where(mr < 16, mr, jnp.where(mr < 20, mr, jnp.where(mr < 24, mr - 4, mr - 24)))
    half_of = jnp.where(mr < 20, 0, 1)
    rowkey = (slot_of + 64 * half_of).astype(F32)
    half_lane = ((iota((1, 128), 1) // 8) % 2 * 64).astype(F32)

    def choose(d):
        cz = cb[d].astype(F32)
        eqs = []
        for k in range(NX):
            g = ((x + k) % NX * NZ + z).astype(F32)
            eqs.append(jnp.where(cz == g, 1.0, 0.0))
        ranks = jnp.dot(jnp.concatenate(eqs, axis=0).astype(BF16), tri,
                        preferred_element_type=F32)
        for k in range(NX):
            hit = jnp.sum(eqs[k], axis=0, keepdims=True)
            rank = jnp.sum(ranks[8 * k:8 * k + 8], axis=0, keepdims=True)
            key = jnp.where(hit > 0.5, rank + half_lane, -1.0)
            hotb[d, 40 * k:40 * k + 40, :] = jnp.where(rowkey == key, 1.0, 0.0).astype(BF16)

    cand_all = rcopy(cb.at[pl.ds(1, 7)], cb.at[pl.ds(1, 7)], cb_s.at[0], cb_r.at[0], zup)
    cand_all.wait_recv()
    for d in range(8):
        choose(d)
    core_cp[3].wait_recv()
    for cp in fin_cp:
        cp.wait_recv()
    pbuf[...] = part[7] + rcore[3] + rfin[0] + rfin[1]

    pt = jnp.concatenate([pbuf[pl.ds(k, 8, stride=24), :] for k in range(24)], axis=0)
    lane = iota((192, 128), 1)
    low = lane < 64
    a2 = jnp.where(low, pltpu.roll(pt, 64, 1), pt)
    a4 = jnp.concatenate([a2, a2], axis=1)
    hi = pt.astype(BF16).astype(F32)
    rest = pt - hi
    mid = rest.astype(BF16).astype(F32)
    lo = rest - mid
    g3 = jnp.concatenate(
        [jnp.where(low, hi, pltpu.roll(mid, 64, 1)), jnp.where(low, lo, 0.0)], axis=1
    ).astype(BF16)
    sq = jnp.zeros((8, 256), F32)
    for m in range(16):
        gx = jnp.dot(g3, expand[:, 256 * m:256 * m + 256], preferred_element_type=F32)
        u = jnp.sum((gx * a4).reshape(24, 8, 256), axis=0)
        ubuf32[:, 256 * m:256 * m + 256] = u
        sq = sq + u * u
    inv = lax.rsqrt(jnp.sum(sq, axis=1, keepdims=True) / 4096.0 + EPS)
    for m in range(16):
        usend[m // 2, 8 * (m % 2):8 * (m % 2) + 8, :] = (
            ubuf32[:, 256 * m:256 * m + 256] * inv
        ).astype(BF16)
    my_rows = pl.ds(pl.multiple_of(t * 16, 16), 16)
    zb[0, my_rows, :] = usend[t]

    def u_cp(d, k):
        to = (t + k) % 8
        return rcopy(usend.at[to], zb.at[d, my_rows, :], u_s.at[d], u_r.at[d],
                     dev(x * NZ + (z + d) % NZ, to))

    near = (0, 1, 7, 2, 6)
    for d in near:
        for k in range(8):
            if (d, k) != (0, 0):
                u_cp(d, k).start()

    def u_all(d):
        n = 7 if d == 0 else 8
        return rcopy(zb.at[d, pl.ds(0, 16 * n)], zb.at[d, pl.ds(0, 16 * n)], u_s.at[d], u_r.at[d], zup)

    def z_in(d):
        return rcopy(zb.at[d], zb.at[d], z_s.at[d], z_r.at[d], zup)

    z_half = [rcopy(zb.at[3, pl.ds(0, 64)], zb.at[4, pl.ds(0, 64)], z_s.at[4], z_r.at[4], zup),
              rcopy(zb.at[5, pl.ds(64, 64)], zb.at[4, pl.ds(64, 64)], z_s.at[0], z_r.at[0], zdn)]
    z_far = [rcopy(zb.at[2], zb.at[3], z_s.at[3], z_r.at[3], zup),
             rcopy(zb.at[6], zb.at[5], z_s.at[5], z_r.at[5], zdn)]

    def x_cp(d, k):
        return rcopy(xs.at[d, k], r.at[0, d, k], x_s.at[0], x_r.at[d],
                     dev((x + k) % NX * NZ + z, t))

    def y_cp(d, k):
        if k == 0:
            return rcopy(r.at[0, d], r.at[2, d], y_s.at[0], y_r.at[0, d], yup)
        if k == 1:
            return rcopy(r.at[0, d], r.at[4, d], y_s.at[1], y_r.at[0, d], ydn)
        if k == 2:
            return rcopy(r.at[2, d, pl.ds(0, 2)], r.at[6, d, pl.ds(0, 2)],
                         y_s.at[2], y_r.at[1, d], yup)
        return rcopy(r.at[4, d, pl.ds(2, 2)], r.at[6, d, pl.ds(2, 2)],
                     y_s.at[2], y_r.at[1, d], ydn)

    def c_cp(d, k):
        return rcopy(r.at[2 * k, d], r.at[2 * k + 1, d], c_s.at[k], c_r.at[d], partner)

    def b_cp(d, k):
        to = (x + NX - k) % NX * NZ + (z + NZ - d) % NZ
        return rcopy(rs.at[d, k], ret.at[d, k], b_s.at[1 if d == 0 else 0], b_r.at[d], dev(to, t))

    def t_cp(k):
        to = x * NZ + (z + (2 if k < 2 else NZ - 2)) % NZ
        return rcopy(rs.at[4, k], tbuf.at[k], b_s.at[0], t_r.at[k], dev(to, t))

    def t_on(k):
        to = (x + NX - k) % NX * NZ + (z + (2 if k < 2 else NZ - 2)) % NZ
        return rcopy(tbuf.at[k], ret.at[4, k], t_s.at[0], b_r.at[4], dev(to, t))

    def own_cp():
        return pltpu.make_async_copy(rs.at[0, 0], ret.at[0, 0], b_s.at[2])

    def pack(d):
        msg = jnp.dot(hotb[d], zb[d], preferred_element_type=F32)
        r[0, d, 0] = msg[0:40].astype(BF16)
        for k in range(1, NX):
            xs[d, k] = msg[40 * k:40 * k + 40].astype(BF16)

    row8 = iota((8, 128), 0)

    def scores(d):
        l0 = jnp.concatenate([r[k, d, :, 0:24, :].reshape(96, 256) for k in range(8)], axis=1)
        l1 = jnp.concatenate([r[k, d, :, 16:40, :].reshape(96, 256) for k in range(8)], axis=1)
        acc0 = lax.dot_general(l0, q0[...], NT, preferred_element_type=F32)
        acc1 = lax.dot_general(l1, q1[...], NT, preferred_element_type=F32)
        for k in range(NX):
            b = 24 * k
            m = acc0[b:b + 16] + acc1[b + 8:b + 24]
            ex = acc0[b + 16:b + 24] + pltpu.roll(acc1[b:b + 8], 4, 0)
            ex2 = pltpu.roll(ex, 4, 0)
            for j in range(5):
                rs[d, k, 16 * j:16 * j + 16, :] = m[:, 128 * j:128 * j + 128].astype(BF16)
            for j in range(3):
                v = ex[:, 128 * j:128 * j + 128]
                if j < 2:
                    v = jnp.where(row8 < 4, v, ex2[:, 128 * j + 384:128 * j + 512])
                rs[d, k, 80 + 8 * j:88 + 8 * j, :] = v.astype(BF16)

    def s1(d):
        pack(d)
        for k in (2, 1, 3):
            x_cp(d, k).start()

    def s2(d):
        rcopy(r.at[0, d, pl.ds(1, 3)], r.at[0, d, pl.ds(1, 3)], x_s.at[0], x_r.at[d], zup).wait_recv()
        y_cp(d, 0).start()
        y_cp(d, 1).start()
        c_cp(d, 0).start()

    def s3(d):
        rcopy(r.at[pl.ds(0, 2), d], r.at[pl.ds(0, 2), d], y_s.at[0], y_r.at[0, d], zup).wait_recv()
        y_cp(d, 2).start()
        y_cp(d, 3).start()
        c_cp(d, 1).start()
        c_cp(d, 2).start()

    def s4(d):
        rcopy(r.at[6, d], r.at[6, d], y_s.at[2], y_r.at[1, d], zup).wait_recv()
        c_cp(d, 3).start()

    def s5(d):
        rcopy(r.at[pl.ds(0, 4), d], r.at[pl.ds(0, 4), d], c_s.at[0], c_r.at[d], zup).wait_recv()
        scores(d)
        for k in range(NX):
            if d == 4:
                t_cp(k).start()
            elif (d, k) == (0, 0):
                own_cp().start()
            else:
                b_cp(d, k).start()

    def u_wait(d):
        u_all(d).wait_recv()

    for d in near:
        u_wait(d)
        if d == 2:
            z_far[0].start()
        if d == 6:
            z_far[1].start()
        s1(d)
    for h, dst in ((0, q0), (1, q1)):
        pltpu.make_async_copy(qh.at[:, pl.ds(0, 2048)], dst, q_sem.at[h]).wait()
    s2(1)
    z_far[0].wait_recv()
    z_half[0].start()
    s1(3)
    z_far[1].wait_recv()
    z_half[1].start()
    s1(5)
    s2(6), s3(1), s2(3)
    z_half[0].wait_recv()
    z_half[1].wait_recv()
    s1(4)
    s3(6), s2(5)
    s4(1), s3(3), s5(1), s2(4)
    s4(6), s3(5), s2(2), s5(6)
    s4(3), s3(4), s2(7), s5(3)
    s4(5), s3(2), s2(0), s4(4), s5(5)
    s3(7), s4(2), s5(4)
    s3(0), s4(7), s5(2)
    s4(0), s5(7)

    def relay(ks):
        for k in ks:
            t_cp(k).wait_recv()
            t_on(k).start()

    relay((2, 3))
    s5(0)
    relay((0, 1))

    def sent():
        for j in range(4):
            core_cp[j].wait_send()
            fin_cp[j].wait_send()
        for j in range(2):
            rel_cp[j].wait_send()
            z_half[j].wait_send()
        for d in near:
            u_all(d).wait_send()
        cand_all.wait_send()
        for cp in z_far:
            cp.wait_send()

        rcopy(xs.at[:, pl.ds(1, 3)], xs.at[:, pl.ds(1, 3)], x_s.at[0], x_r.at[0], zup).wait_send()
        for k in range(3):
            rcopy(r.at[k], r.at[k], y_s.at[k], y_r.at[0, 0], zup).wait_send()
        for k in range(4):
            rcopy(r.at[k], r.at[k], c_s.at[k], c_r.at[0], zup).wait_send()

    sent()

    def got(d):
        if d == 0:
            own_cp().wait()
            some = ret.at[0, pl.ds(1, 3)]
        else:
            some = ret.at[d]
        rcopy(some, some, b_s.at[0], b_r.at[d], zup).wait_recv()

    for d in (1, 6, 3, 5, 2, 7, 0, 4):
        got(d)

    def returned():
        some = rs.at[pl.ds(1, 7)]
        rcopy(some, some, b_s.at[0], b_r.at[1], zup).wait_send()
        some = rs.at[0, pl.ds(1, 3)]
        rcopy(some, some, b_s.at[1], b_r.at[0], zup).wait_send()
        rcopy(tbuf, tbuf, t_s.at[0], t_r.at[0], zup).wait_send()

    returned()


def pick_kernel(cand, ret, out):
    dp = lax.axis_index("dp")
    cd = cand[...]
    rel = ((cd % NZ - dp % NZ + NZ) % NZ * NX + (cd // NZ - dp // NZ + NX) % NX).astype(F32)
    group = iota((32, 64), 0).astype(F32)
    hit = jnp.zeros((32, 64), F32)
    for k in range(4):
        hit = hit + jnp.where(rel[k:k + 1, :] == group, 1.0, 0.0)
    tri = jnp.where(iota((64, 256), 0) < iota((64, 256), 1) % 64, 1.0, 0.0).astype(BF16)
    rank = jnp.dot(hit.astype(BF16), tri, preferred_element_type=F32)
    lane = iota((64, 256), 1)
    dup = jnp.where(iota((64, 256), 0) == lane % 64, 1.0, 0.0).astype(BF16)
    wide = jnp.dot(rel.astype(BF16), dup, preferred_element_type=F32)
    flat = jnp.sum(jnp.where(iota((4, 256), 0) == iota((4, 256), 1) // 64, wide, 0.0),
                   axis=0, keepdims=True)
    mine = jnp.where(flat == iota((32, 256), 0).astype(F32), rank, 0.0)
    slot = jnp.sum(mine, axis=0, keepdims=True)
    rows = jnp.concatenate([flat, slot, jnp.zeros((6, 256), F32)], axis=0).astype(BF16)
    eye = jnp.where(iota((8, 128), 0) == iota((8, 128), 1), 1.0, 0.0).astype(BF16)
    cols = lax.dot_general(rows, eye, (((0,), (0,)), ((), ())), preferred_element_type=F32)
    relc, slotc = cols[:, 0:1], cols[:, 1:2]
    key = jnp.where(slotc < 15.5, relc * 16.0 + slotc, -1.0)
    key0 = jnp.where(slotc > 15.5, relc * 8.0 + slotc - 16.0, -1.0)
    key1 = jnp.where(slotc > 15.5, relc * 8.0 + slotc - 12.0, -1.0)
    at512 = iota((256, 512), 1).astype(F32)
    at256 = iota((256, 256), 1).astype(F32)
    hot = jnp.where(at512 == key, 1.0, 0.0).astype(BF16)
    hot0 = jnp.where(at256 == key0, 1.0, 0.0).astype(BF16)
    hot1 = jnp.where(at256 == key1, 1.0, 0.0).astype(BF16)
    for js, more in (((0, 1, 2), hot0), ((3, 4), hot1)):
        pick = jnp.concatenate([hot, more], axis=1)
        vals = jnp.concatenate(
            [jnp.concatenate([
                ret[:, :, 16 * j:16 * j + 16, :].reshape(512, 128),
                ret[:, :, 80 + 8 * (j % 3):88 + 8 * (j % 3), :].reshape(256, 128),
            ], axis=0) for j in js], axis=1)
        res = jnp.dot(pick, vals, preferred_element_type=F32)
        for k in range(4):
            out[:, k, 128 * js[0]:128 * js[-1] + 128] = res[64 * k:64 * k + 64]


def local(activations, out_grads, proj_in, proj_out, queries, candidates):
    cand_t = candidates.T
    vm = pl.BlockSpec(memory_space=pltpu.VMEM)
    hbm = pl.BlockSpec(memory_space=pl.ANY)
    dma = pltpu.SemaphoreType.DMA
    ret = pl.pallas_call(
        main_kernel,
        name="attribution",
        out_shape=jax.ShapeDtypeStruct((8, 4, 104, 128), BF16),
        in_specs=[hbm] * 6,
        out_specs=hbm,
        scratch_shapes=[
            pltpu.VMEM((4, 384, 1792), BF16),
            pltpu.VMEM((4, 384, 512), BF16),
            pltpu.VMEM((128, 1792), BF16),
            pltpu.VMEM((128, 512), BF16),
            pltpu.VMEM((256, 4096), BF16),
            pltpu.VMEM((8, 192, 128), F32),
            pltpu.VMEM((4, 192, 128), F32),
            pltpu.VMEM((192, 128), F32),
            pltpu.VMEM((2, 96, 128), F32),
            pltpu.VMEM((2, 192, 128), F32),
            pltpu.VMEM((2, 192, 128), F32),
            pltpu.VMEM((192, 128), F32),
            pltpu.VMEM((8, 4096), F32),
            pltpu.VMEM((8, 16, 256), BF16),
            pltpu.VMEM((8, 128, 256), BF16),
            pltpu.VMEM((8, 8, 128), BF16),
            pltpu.VMEM((8, 160, 128), BF16),
            pltpu.VMEM((8, 4, 40, 256), BF16),
            pltpu.VMEM((8, 8, 4, 40, 256), BF16),
            pltpu.VMEM((640, 2048), BF16),
            pltpu.VMEM((640, 2048), BF16),
            pltpu.VMEM((8, 4, 104, 128), BF16),
            pltpu.VMEM((4, 104, 128), BF16),
            pltpu.VMEM((4, 64), I32),
            dma((4,)), dma((4,)), dma((2,)), dma((3,)),
            dma((1,)), dma((1,)), dma((4,)), dma((4,)), dma((2,)), dma((2,)), dma((4,)), dma((4,)),
            dma((8,)), dma((8,)), dma((8,)), dma((8,)), dma((1,)), dma((8,)), dma((3,)), dma((2, 8)),
            dma((4,)), dma((8,)), dma((3,)), dma((8,)), dma((1,)), dma((4,)),
        ],
        compiler_params=pltpu.CompilerParams(
            collective_id=0, has_side_effects=True, vmem_limit_bytes=56 * 1024 * 1024
        ),
    )(
        activations.reshape(1536, 1792), out_grads.reshape(1536, 512),
        proj_in.T, proj_out.T, queries[0], cand_t,
    )
    return pl.pallas_call(
        pick_kernel,
        name="pick",
        out_shape=jax.ShapeDtypeStruct((64, 4, 640), F32),
        in_specs=[vm, vm],
        out_specs=vm,
    )(cand_t, ret)


def solution(mesh):
    placed = (
        P("dp", None, "tensor"),
        P("dp", None, "tensor"),
        P("tensor", None),
        P("tensor", None),
        P("dp", "tensor", None),
        P("dp", None),
    )
    return jax.shard_map(
        local, mesh=mesh, in_specs=placed, out_specs=P("dp", None, "tensor"), check_vma=False
    )
```

```python
import jax
import jax.numpy as jnp
from jax import lax
from jax.experimental import pallas as pl
from jax.experimental.pallas import tpu as pltpu
from jax.sharding import PartitionSpec as P

EPS = 1e-06
NX, NZ, NY = 4, 8, 4
F32, BF16, I32 = jnp.float32, jnp.bfloat16, jnp.int32
NT = (((1,), (1,)), ((), ()))


def iota(shape, axis):
    return lax.broadcasted_iota(I32, shape, axis)


def main_kernel(
    act, og, pin, pout, qh, cand, ret,
    abuf, obuf, wa, wo, expand, part, rcore, csum, rrel, fin, rfin, pbuf, ubuf32, usend,
    zb, cb, hotb, xs, r, q0, q1, rs, tbuf,
    cbuf, act_sem, og_sem, q_sem, w_sem,
    cb_s, cb_r, core_s, core_r, rel_s, rel_r, fin_s, fin_r, u_s, u_r,
    z_s, z_r, x_s, x_r, y_s, y_r, c_s, c_r, b_s, b_r, t_s, t_r,
):
    dp = lax.axis_index("dp")
    t = lax.axis_index("tensor")
    x, z = dp // NZ, dp % NZ
    y, c = t // 2, t % 2

    def dev(dp_to, t_to):
        return {"dp": dp_to, "tensor": t_to}

    def rcopy(src, dst, ss, rr, to):
        return pltpu.make_async_remote_copy(
            src_ref=src, dst_ref=dst, send_sem=ss, recv_sem=rr,
            device_id=to, device_id_type=pl.DeviceIdType.MESH,
        )

    partner = dev(dp, 2 * y + (1 - c))
    yup = dev(dp, 2 * ((y + 1) % NY) + c)
    ydn = dev(dp, 2 * ((y + NY - 1) % NY) + c)
    zup = dev(x * NZ + (z + 1) % NZ, t)
    zdn = dev(x * NZ + (z + NZ - 1) % NZ, t)

    barrier = pltpu.get_barrier_semaphore()

    def greet(to):
        pl.semaphore_signal(barrier, inc=1, device_id=to, device_id_type=pl.DeviceIdType.MESH)

    for k in range(1, 8):
        greet(dev(dp, (t + k) % 8))
    for d in (1, 2, 6, 7):
        for k in range(8):
            greet(dev(x * NZ + (z + d) % NZ, (t + k) % 8))
    for d in (3, 4, 5):
        greet(dev(x * NZ + (z + d) % NZ, t))
    for k in range(1, NX):
        greet(dev((x + k) % NX * NZ + z, t))

    ys = [(y + 2) % NY, (y + 1) % NY, (y + 3) % NY, y]

    def load(j):
        for n in (2 * j, 2 * j + 1):
            tb = 2 * ys[j] + ((1 - c) if n % 2 == 0 else c)
            rows = pl.ds(pl.multiple_of(tb * 192, 192), 192)
            part_rows = pl.ds(n % 2 * 192, 192)
            pltpu.make_async_copy(act.at[rows, :], abuf.at[j, part_rows], act_sem.at[j]).start()
            pltpu.make_async_copy(og.at[rows, :], obuf.at[j, part_rows], og_sem.at[j]).start()

    small = [
        pltpu.make_async_copy(pin, wa.at[pl.ds(64, 64)], w_sem.at[0]),
        pltpu.make_async_copy(pout, wo.at[pl.ds(0, 64)], w_sem.at[1]),
        pltpu.make_async_copy(cand, cbuf, w_sem.at[2]),
    ]
    for cp in small:
        cp.start()
    load(0)
    load(1)

    wa[0:64, :] = jnp.zeros((64, wa.shape[1]), BF16)
    wo[64:128, :] = jnp.zeros((64, wo.shape[1]), BF16)
    small[0].wait()
    small[1].wait()

    def project(j):
        pltpu.make_async_copy(act.at[pl.ds(0, 384), :], abuf.at[j], act_sem.at[j]).wait()
        pltpu.make_async_copy(og.at[pl.ds(0, 384), :], obuf.at[j], og_sem.at[j]).wait()
        if j < 2:
            load(j + 2)
        both = lax.dot_general(
            abuf[j], wa[...], NT, preferred_element_type=F32
        ) + lax.dot_general(obuf[j], wo[...], NT, preferred_element_type=F32)
        part[2 * j] = both[0:192]
        part[2 * j + 1] = both[192:384]

    core_cp = [rcopy(part.at[2 * j], rcore.at[j], core_s.at[0], core_r.at[j], partner)
               for j in range(4)]
    rel_cp = [rcopy(csum.at[pl.ds(0, 96)], rrel.at[0], rel_s.at[0], rel_r.at[0], yup),
              rcopy(csum.at[pl.ds(96, 96)], rrel.at[1], rel_s.at[0], rel_r.at[1], ydn)]
    top, low_half = pl.ds(0, 96), pl.ds(96, 96)

    def fin_copy(j, early):
        rows = (low_half if early else top) if j == 0 else (top if early else low_half)
        n = 2 * j + (0 if early else 1)
        return rcopy(fin.at[j, rows], rfin.at[j, rows], fin_s.at[0], fin_r.at[n],
                     yup if j == 0 else ydn)

    fin_cp = [fin_copy(j, early) for j in (0, 1) for early in (True, False)]

    def cand_cp(d):
        return rcopy(cb.at[0], cb.at[d], cb_s.at[0], cb_r.at[0], dev(x * NZ + (z + d) % NZ, t))

    project(0)
    pl.semaphore_wait(barrier, 7 + 32 + 3 + NX - 1)
    core_cp[0].start()
    project(1)
    core_cp[1].start()
    core_cp[0].wait_recv()
    csum[...] = part[1] + rcore[0]
    rel_cp[0].start()
    rel_cp[1].start()
    small[2].wait()
    e_of = iota((64, 128), 1) // 16 * 8 + iota((64, 128), 1) % 8
    dup = jnp.where(iota((64, 128), 0) == e_of, 1.0, 0.0).astype(BF16)
    c2 = jnp.dot(cbuf[...].astype(F32).astype(BF16), dup, preferred_element_type=F32)
    cb[0] = jnp.concatenate([c2, jnp.full((4, 128), -1.0, F32)], axis=0).astype(BF16)

    for d in range(1, 8):
        cand_cp(d).start()
    project(2)
    core_cp[2].start()
    core_cp[1].wait_recv()
    fin[0, 96:192] = part[3, 96:192] + rcore[1, 96:192]
    fin_cp[0].start()
    project(3)
    core_cp[3].start()
    core_cp[2].wait_recv()
    fin[1, 0:96] = part[5, 0:96] + rcore[2, 0:96]
    fin_cp[2].start()

    rel_y = [y, (y + 3) % NY, (y + 1) % NY, (y + 2) % NY]
    for rel in range(8):
        ts = 2 * rel_y[rel // 2] + (c if rel % 2 == 0 else 1 - c)
        for h, dst in ((0, q0), (1, q1)):
            cols = pl.ds(pl.multiple_of(ts * 512 + h * 256, 256), 256)
            cp = pltpu.make_async_copy(
                qh.at[:, cols], dst.at[:, pl.ds(rel * 256, 256)], q_sem.at[h]
            )
            cp.start()

    row = iota((256, 4096), 0)
    col = iota((256, 4096), 1)
    expand[...] = jnp.where((row % 64 == col // 64) & (row < 192), 1.0, 0.0).astype(BF16)
    rel_cp[0].wait_recv()
    fin[0, 0:96] = part[3, 0:96] + rcore[1, 0:96] + rrel[0]
    fin_cp[1].start()
    rel_cp[1].wait_recv()
    fin[1, 96:192] = part[5, 96:192] + rcore[2, 96:192] + rrel[1]
    fin_cp[3].start()
    tri_r, tri_c = iota((128, 128), 0), iota((128, 128), 1)
    tri = jnp.where(
        ((tri_r // 8) % 2 == 0)
        & (tri_r // 16 * 8 + tri_r % 8 < tri_c // 16 * 8 + tri_c % 8), 1.0, 0.0
    ).astype(BF16)
    mr = iota((40, 128), 0)
    slot_of = jnp.where(mr < 16, mr, jnp.where(mr < 20, mr, jnp.where(mr < 24, mr - 4, mr - 24)))
    half_of = jnp.where(mr < 20, 0, 1)
    rowkey = (slot_of + 64 * half_of).astype(F32)
    half_lane = ((iota((1, 128), 1) // 8) % 2 * 64).astype(F32)

    def choose(d):
        cz = cb[d].astype(F32)
        eqs = []
        for k in range(NX):
            g = ((x + k) % NX * NZ + z).astype(F32)
            eqs.append(jnp.where(cz == g, 1.0, 0.0))
        ranks = jnp.dot(jnp.concatenate(eqs, axis=0).astype(BF16), tri,
                        preferred_element_type=F32)
        for k in range(NX):
            hit = jnp.sum(eqs[k], axis=0, keepdims=True)
            rank = jnp.sum(ranks[8 * k:8 * k + 8], axis=0, keepdims=True)
            key = jnp.where(hit > 0.5, rank + half_lane, -1.0)
            hotb[d, 40 * k:40 * k + 40, :] = jnp.where(rowkey == key, 1.0, 0.0).astype(BF16)

    cand_all = rcopy(cb.at[pl.ds(1, 7)], cb.at[pl.ds(1, 7)], cb_s.at[0], cb_r.at[0], zup)
    cand_all.wait_recv()
    for d in range(8):
        choose(d)
    core_cp[3].wait_recv()
    for cp in fin_cp:
        cp.wait_recv()
    pbuf[...] = part[7] + rcore[3] + rfin[0] + rfin[1]

    pt = jnp.concatenate([pbuf[pl.ds(k, 8, stride=24), :] for k in range(24)], axis=0)
    lane = iota((192, 128), 1)
    low = lane < 64
    a2 = jnp.where(low, pltpu.roll(pt, 64, 1), pt)
    a4 = jnp.concatenate([a2, a2], axis=1)
    hi = pt.astype(BF16).astype(F32)
    rest = pt - hi
    mid = rest.astype(BF16).astype(F32)
    lo = rest - mid
    g3 = jnp.concatenate(
        [jnp.where(low, hi, pltpu.roll(mid, 64, 1)), jnp.where(low, lo, 0.0)], axis=1
    ).astype(BF16)
    sq = jnp.zeros((8, 256), F32)
    for m in range(16):
        gx = jnp.dot(g3, expand[:, 256 * m:256 * m + 256], preferred_element_type=F32)
        u = jnp.sum((gx * a4).reshape(24, 8, 256), axis=0)
        ubuf32[:, 256 * m:256 * m + 256] = u
        sq = sq + u * u
    inv = lax.rsqrt(jnp.sum(sq, axis=1, keepdims=True) / 4096.0 + EPS)
    for m in range(16):
        usend[m // 2, 8 * (m % 2):8 * (m % 2) + 8, :] = (
            ubuf32[:, 256 * m:256 * m + 256] * inv
        ).astype(BF16)
    my_rows = pl.ds(pl.multiple_of(t * 16, 16), 16)
    zb[0, my_rows, :] = usend[t]

    near = (0, 1, 7, 2, 6)

    def u_cp(d, k):
        to = (t + k) % 8
        return rcopy(usend.at[to], zb.at[d, my_rows, :], u_s.at[min(d, 1)], u_r.at[near.index(d)],
                     dev(x * NZ + (z + d) % NZ, to))

    for d in near:
        for k in range(8):
            if (d, k) != (0, 0):
                u_cp(d, k).start()

    def u_all(d):
        n = 7 if d == 0 else 8
        return rcopy(zb.at[d, pl.ds(0, 16 * n)], zb.at[d, pl.ds(0, 16 * n)],
                     u_s.at[min(d, 1)], u_r.at[near.index(d)], zup)

    z_half = [rcopy(zb.at[3, pl.ds(0, 64)], zb.at[4, pl.ds(0, 64)], z_s.at[0], z_r.at[0], zup),
              rcopy(zb.at[5, pl.ds(64, 64)], zb.at[4, pl.ds(64, 64)], z_s.at[1], z_r.at[1], zdn)]
    z_far = [rcopy(zb.at[2], zb.at[3], z_s.at[2], z_r.at[2], zup),
             rcopy(zb.at[6], zb.at[5], z_s.at[3], z_r.at[3], zdn)]

    def x_cp(d, k):
        return rcopy(xs.at[d, k], r.at[0, d, k], x_s.at[0], x_r.at[d],
                     dev((x + k) % NX * NZ + z, t))

    def y_cp(d, k):
        if k == 0:
            return rcopy(r.at[0, d], r.at[2, d], y_s.at[0], y_r.at[0, d], yup)
        if k == 1:
            return rcopy(r.at[0, d], r.at[4, d], y_s.at[1], y_r.at[0, d], ydn)
        if k == 2:
            return rcopy(r.at[2, d, pl.ds(0, 2)], r.at[6, d, pl.ds(0, 2)],
                         y_s.at[2], y_r.at[1, d], yup)
        return rcopy(r.at[4, d, pl.ds(2, 2)], r.at[6, d, pl.ds(2, 2)],
                     y_s.at[2], y_r.at[1, d], ydn)

    def c_cp(d, k):
        return rcopy(r.at[2 * k, d], r.at[2 * k + 1, d], c_s.at[k], c_r.at[d], partner)

    def b_cp(d, k):
        to = (x + NX - k) % NX * NZ + (z + NZ - d) % NZ
        return rcopy(rs.at[d, k], ret.at[d, k], b_s.at[1 if d == 0 else 0], b_r.at[d], dev(to, t))

    def t_cp(k):
        to = x * NZ + (z + (2 if k < 2 else NZ - 2)) % NZ
        return rcopy(rs.at[4, k], tbuf.at[k], b_s.at[0], t_r.at[k], dev(to, t))

    def t_on(k):
        to = (x + NX - k) % NX * NZ + (z + (2 if k < 2 else NZ - 2)) % NZ
        return rcopy(tbuf.at[k], ret.at[4, k], t_s.at[0], b_r.at[4], dev(to, t))

    def own_cp():
        return pltpu.make_async_copy(rs.at[0, 0], ret.at[0, 0], b_s.at[2])

    def pack(d):
        msg = jnp.dot(hotb[d], zb[d], preferred_element_type=F32)
        r[0, d, 0] = msg[0:40].astype(BF16)
        for k in range(1, NX):
            xs[d, k] = msg[40 * k:40 * k + 40].astype(BF16)

    row8 = iota((8, 128), 0)

    def scores(d):
        l0 = jnp.concatenate([r[k, d, :, 0:24, :].reshape(96, 256) for k in range(8)], axis=1)
        l1 = jnp.concatenate([r[k, d, :, 16:40, :].reshape(96, 256) for k in range(8)], axis=1)
        acc0 = lax.dot_general(l0, q0[...], NT, preferred_element_type=F32)
        acc1 = lax.dot_general(l1, q1[...], NT, preferred_element_type=F32)
        for k in range(NX):
            b = 24 * k
            m = acc0[b:b + 16] + acc1[b + 8:b + 24]
            ex = acc0[b + 16:b + 24] + pltpu.roll(acc1[b:b + 8], 4, 0)
            ex2 = pltpu.roll(ex, 4, 0)
            for j in range(5):
                rs[d, k, 16 * j:16 * j + 16, :] = m[:, 128 * j:128 * j + 128].astype(BF16)
            for j in range(3):
                v = ex[:, 128 * j:128 * j + 128]
                if j < 2:
                    v = jnp.where(row8 < 4, v, ex2[:, 128 * j + 384:128 * j + 512])
                rs[d, k, 80 + 8 * j:88 + 8 * j, :] = v.astype(BF16)

    def s1(d):
        pack(d)
        for k in (2, 1, 3):
            x_cp(d, k).start()

    def s2(d):
        rcopy(r.at[0, d, pl.ds(1, 3)], r.at[0, d, pl.ds(1, 3)], x_s.at[0], x_r.at[d], zup).wait_recv()
        y_cp(d, 0).start()
        y_cp(d, 1).start()
        c_cp(d, 0).start()

    def s3(d):
        rcopy(r.at[pl.ds(0, 2), d], r.at[pl.ds(0, 2), d], y_s.at[0], y_r.at[0, d], zup).wait_recv()
        y_cp(d, 2).start()
        y_cp(d, 3).start()
        c_cp(d, 1).start()
        c_cp(d, 2).start()

    def s4(d):
        rcopy(r.at[6, d], r.at[6, d], y_s.at[2], y_r.at[1, d], zup).wait_recv()
        c_cp(d, 3).start()

    def s5(d):
        rcopy(r.at[pl.ds(0, 4), d], r.at[pl.ds(0, 4), d], c_s.at[0], c_r.at[d], zup).wait_recv()
        scores(d)
        for k in range(NX):
            if d == 4:
                t_cp(k).start()
            elif (d, k) == (0, 0):
                own_cp().start()
            else:
                b_cp(d, k).start()

    def u_wait(d):
        u_all(d).wait_recv()

    for d in near:
        u_wait(d)
        if d == 2:
            z_far[0].start()
        if d == 6:
            z_far[1].start()
        s1(d)
    for h, dst in ((0, q0), (1, q1)):
        pltpu.make_async_copy(qh.at[:, pl.ds(0, 2048)], dst, q_sem.at[h]).wait()
    s2(1)
    z_far[0].wait_recv()
    z_half[0].start()
    s1(3)
    z_far[1].wait_recv()
    z_half[1].start()
    s1(5)
    s2(6), s3(1), s2(3)
    z_half[0].wait_recv()
    z_half[1].wait_recv()
    s1(4)
    s3(6), s2(5)
    s4(1), s3(3), s5(1), s2(4)
    s4(6), s3(5), s2(2), s5(6)
    s4(3), s3(4), s2(7), s5(3)
    s4(5), s3(2), s2(0), s4(4), s5(5)
    s3(7), s4(2), s5(4)
    s3(0), s4(7), s5(2)
    s4(0), s5(7)

    def relay(ks):
        for k in ks:
            t_cp(k).wait_recv()
            t_on(k).start()

    relay((2, 3))
    s5(0)
    relay((0, 1))

    def sent():
        rcopy(rcore, rcore, core_s.at[0], core_r.at[0], zup).wait_send()
        rcopy(fin, fin, fin_s.at[0], fin_r.at[0], zup).wait_send()
        rcopy(csum, csum, rel_s.at[0], rel_r.at[0], zup).wait_send()
        for j in range(2):
            z_half[j].wait_send()
        u_all(0).wait_send()
        rcopy(zb.at[pl.ds(0, 4)], zb.at[pl.ds(0, 4)], u_s.at[1], u_r.at[0], zup).wait_send()
        cand_all.wait_send()
        for cp in z_far:
            cp.wait_send()

        rcopy(xs.at[:, pl.ds(1, 3)], xs.at[:, pl.ds(1, 3)], x_s.at[0], x_r.at[0], zup).wait_send()
        for k in range(3):
            rcopy(r.at[k], r.at[k], y_s.at[k], y_r.at[0, 0], zup).wait_send()
        for k in range(4):
            rcopy(r.at[k], r.at[k], c_s.at[k], c_r.at[0], zup).wait_send()

    sent()

    def got(d):
        if d == 0:
            own_cp().wait()
            some = ret.at[0, pl.ds(1, 3)]
        else:
            some = ret.at[d]
        rcopy(some, some, b_s.at[0], b_r.at[d], zup).wait_recv()

    for d in (1, 6, 3, 5, 2, 7, 0, 4):
        got(d)

    def returned():
        some = rs.at[pl.ds(1, 7)]
        rcopy(some, some, b_s.at[0], b_r.at[1], zup).wait_send()
        some = rs.at[0, pl.ds(1, 3)]
        rcopy(some, some, b_s.at[1], b_r.at[0], zup).wait_send()
        rcopy(tbuf, tbuf, t_s.at[0], t_r.at[0], zup).wait_send()

    returned()


def pick_kernel(cand, ret, out):
    dp = lax.axis_index("dp")
    cd = cand[...]
    rel = ((cd % NZ - dp % NZ + NZ) % NZ * NX + (cd // NZ - dp // NZ + NX) % NX).astype(F32)
    group = iota((32, 64), 0).astype(F32)
    hit = jnp.zeros((32, 64), F32)
    for k in range(4):
        hit = hit + jnp.where(rel[k:k + 1, :] == group, 1.0, 0.0)
    tri = jnp.where(iota((64, 256), 0) < iota((64, 256), 1) % 64, 1.0, 0.0).astype(BF16)
    rank = jnp.dot(hit.astype(BF16), tri, preferred_element_type=F32)
    lane = iota((64, 256), 1)
    dup = jnp.where(iota((64, 256), 0) == lane % 64, 1.0, 0.0).astype(BF16)
    wide = jnp.dot(rel.astype(BF16), dup, preferred_element_type=F32)
    flat = jnp.sum(jnp.where(iota((4, 256), 0) == iota((4, 256), 1) // 64, wide, 0.0),
                   axis=0, keepdims=True)
    mine = jnp.where(flat == iota((32, 256), 0).astype(F32), rank, 0.0)
    slot = jnp.sum(mine, axis=0, keepdims=True)
    rows = jnp.concatenate([flat, slot, jnp.zeros((6, 256), F32)], axis=0).astype(BF16)
    eye = jnp.where(iota((8, 128), 0) == iota((8, 128), 1), 1.0, 0.0).astype(BF16)
    cols = lax.dot_general(rows, eye, (((0,), (0,)), ((), ())), preferred_element_type=F32)
    relc, slotc = cols[:, 0:1], cols[:, 1:2]
    key = jnp.where(slotc < 15.5, relc * 16.0 + slotc, -1.0)
    key0 = jnp.where(slotc > 15.5, relc * 8.0 + slotc - 16.0, -1.0)
    key1 = jnp.where(slotc > 15.5, relc * 8.0 + slotc - 12.0, -1.0)
    at512 = iota((256, 512), 1).astype(F32)
    at256 = iota((256, 256), 1).astype(F32)
    hot = jnp.where(at512 == key, 1.0, 0.0).astype(BF16)
    hot0 = jnp.where(at256 == key0, 1.0, 0.0).astype(BF16)
    hot1 = jnp.where(at256 == key1, 1.0, 0.0).astype(BF16)
    for js, more in (((0, 1, 2), hot0), ((3, 4), hot1)):
        pick = jnp.concatenate([hot, more], axis=1)
        vals = jnp.concatenate(
            [jnp.concatenate([
                ret[:, :, 16 * j:16 * j + 16, :].reshape(512, 128),
                ret[:, :, 80 + 8 * (j % 3):88 + 8 * (j % 3), :].reshape(256, 128),
            ], axis=0) for j in js], axis=1)
        res = jnp.dot(pick, vals, preferred_element_type=F32)
        for k in range(4):
            out[:, k, 128 * js[0]:128 * js[-1] + 128] = res[64 * k:64 * k + 64]


def local(activations, out_grads, proj_in, proj_out, queries, candidates):
    cand_t = candidates.T
    vm = pl.BlockSpec(memory_space=pltpu.VMEM)
    hbm = pl.BlockSpec(memory_space=pl.ANY)
    dma = pltpu.SemaphoreType.DMA
    ret = pl.pallas_call(
        main_kernel,
        name="attribution",
        out_shape=jax.ShapeDtypeStruct((8, 4, 104, 128), BF16),
        in_specs=[hbm] * 6,
        out_specs=hbm,
        scratch_shapes=[
            pltpu.VMEM((4, 384, 1792), BF16),
            pltpu.VMEM((4, 384, 512), BF16),
            pltpu.VMEM((128, 1792), BF16),
            pltpu.VMEM((128, 512), BF16),
            pltpu.VMEM((256, 4096), BF16),
            pltpu.VMEM((8, 192, 128), F32),
            pltpu.VMEM((4, 192, 128), F32),
            pltpu.VMEM((192, 128), F32),
            pltpu.VMEM((2, 96, 128), F32),
            pltpu.VMEM((2, 192, 128), F32),
            pltpu.VMEM((2, 192, 128), F32),
            pltpu.VMEM((192, 128), F32),
            pltpu.VMEM((8, 4096), F32),
            pltpu.VMEM((8, 16, 256), BF16),
            pltpu.VMEM((8, 128, 256), BF16),
            pltpu.VMEM((8, 8, 128), BF16),
            pltpu.VMEM((8, 160, 128), BF16),
            pltpu.VMEM((8, 4, 40, 256), BF16),
            pltpu.VMEM((8, 8, 4, 40, 256), BF16),
            pltpu.VMEM((640, 2048), BF16),
            pltpu.VMEM((640, 2048), BF16),
            pltpu.VMEM((8, 4, 104, 128), BF16),
            pltpu.VMEM((4, 104, 128), BF16),
            pltpu.VMEM((4, 64), I32),
            dma((4,)), dma((4,)), dma((2,)), dma((3,)),
            dma((1,)), dma((1,)), dma((1,)), dma((4,)), dma((1,)), dma((2,)), dma((1,)), dma((4,)),
            dma((2,)), dma((5,)), dma((4,)), dma((4,)), dma((1,)), dma((8,)), dma((3,)), dma((2, 8)),
            dma((4,)), dma((8,)), dma((3,)), dma((8,)), dma((1,)), dma((4,)),
        ],
        compiler_params=pltpu.CompilerParams(
            collective_id=0, has_side_effects=True, vmem_limit_bytes=56 * 1024 * 1024
        ),
    )(
        activations.reshape(1536, 1792), out_grads.reshape(1536, 512),
        proj_in.T, proj_out.T, queries[0], cand_t,
    )
    return pl.pallas_call(
        pick_kernel,
        name="pick",
        out_shape=jax.ShapeDtypeStruct((64, 4, 640), F32),
        in_specs=[vm, vm],
        out_specs=vm,
    )(cand_t, ret)


def solution(mesh):
    placed = (
        P("dp", None, "tensor"),
        P("dp", None, "tensor"),
        P("tensor", None),
        P("tensor", None),
        P("dp", "tensor", None),
        P("dp", None),
    )
    return jax.shard_map(
        local, mesh=mesh, in_specs=placed, out_specs=P("dp", None, "tensor"), check_vma=False
    )
```

```python
import jax
import jax.numpy as jnp
from jax import lax
from jax.experimental import pallas as pl
from jax.experimental.pallas import tpu as pltpu
from jax.sharding import PartitionSpec as P

EPS = 1e-06
NX, NZ, NY = 4, 8, 4
F32, BF16, I32 = jnp.float32, jnp.bfloat16, jnp.int32
NT = (((1,), (1,)), ((), ()))


def iota(shape, axis):
    return lax.broadcasted_iota(I32, shape, axis)


def main_kernel(
    act, og, pin, pout, qh, cand, ret,
    abuf, obuf, wa, wo, expand, part, rcore, csum, rrel, fin, rfin, pbuf, ubuf32, usend,
    zb, cb, hotb, xs, r, q0, q1, rs, tbuf,
    cbuf, act_sem, og_sem, q_sem, w_sem,
    cb_s, cb_r, core_s, core_r, rel_s, rel_r, fin_s, fin_r, u_s, u_r,
    z_s, z_r, x_s, x_r, y_s, y_r, c_s, c_r, b_s, b_r, t_s, t_r,
):
    dp = lax.axis_index("dp")
    t = lax.axis_index("tensor")
    x, z = dp // NZ, dp % NZ
    y, c = t // 2, t % 2

    def dev(dp_to, t_to):
        return {"dp": dp_to, "tensor": t_to}

    def rcopy(src, dst, ss, rr, to):
        return pltpu.make_async_remote_copy(
            src_ref=src, dst_ref=dst, send_sem=ss, recv_sem=rr,
            device_id=to, device_id_type=pl.DeviceIdType.MESH,
        )

    partner = dev(dp, 2 * y + (1 - c))
    yup = dev(dp, 2 * ((y + 1) % NY) + c)
    ydn = dev(dp, 2 * ((y + NY - 1) % NY) + c)
    zup = dev(x * NZ + (z + 1) % NZ, t)
    zdn = dev(x * NZ + (z + NZ - 1) % NZ, t)

    barrier = pltpu.get_barrier_semaphore()

    def greet(to):
        pl.semaphore_signal(barrier, inc=1, device_id=to, device_id_type=pl.DeviceIdType.MESH)

    for k in range(1, 8):
        greet(dev(dp, (t + k) % 8))
    for d in (1, 2, 6, 7):
        for k in range(8):
            greet(dev(x * NZ + (z + d) % NZ, (t + k) % 8))
    for d in (3, 4, 5):
        greet(dev(x * NZ + (z + d) % NZ, t))
    for k in range(1, NX):
        greet(dev((x + k) % NX * NZ + z, t))

    ys = [(y + 2) % NY, (y + 1) % NY, (y + 3) % NY, y]

    def load(j):
        for n in (2 * j, 2 * j + 1):
            tb = 2 * ys[j] + ((1 - c) if n % 2 == 0 else c)
            rows = pl.ds(pl.multiple_of(tb * 192, 192), 192)
            part_rows = pl.ds(n % 2 * 192, 192)
            pltpu.make_async_copy(act.at[rows, :], abuf.at[j, part_rows], act_sem.at[j]).start()
            pltpu.make_async_copy(og.at[rows, :], obuf.at[j, part_rows], og_sem.at[j]).start()

    small = [
        pltpu.make_async_copy(pin, wa.at[pl.ds(64, 64)], w_sem.at[0]),
        pltpu.make_async_copy(pout, wo.at[pl.ds(0, 64)], w_sem.at[1]),
        pltpu.make_async_copy(cand, cbuf, w_sem.at[2]),
    ]
    for cp in small:
        cp.start()
    load(0)
    load(1)

    wa[0:64, :] = jnp.zeros((64, wa.shape[1]), BF16)
    wo[64:128, :] = jnp.zeros((64, wo.shape[1]), BF16)
    small[0].wait()
    small[1].wait()

    def project(j):
        pltpu.make_async_copy(act.at[pl.ds(0, 384), :], abuf.at[j], act_sem.at[j]).wait()
        pltpu.make_async_copy(og.at[pl.ds(0, 384), :], obuf.at[j], og_sem.at[j]).wait()
        if j < 2:
            load(j + 2)
        both = lax.dot_general(
            abuf[j], wa[...], NT, preferred_element_type=F32
        ) + lax.dot_general(obuf[j], wo[...], NT, preferred_element_type=F32)
        part[2 * j] = both[0:192]
        part[2 * j + 1] = both[192:384]

    core_cp = [rcopy(part.at[2 * j], rcore.at[j], core_s.at[0], core_r.at[j], partner)
               for j in range(4)]
    rel_cp = [rcopy(csum.at[pl.ds(0, 96)], rrel.at[0], rel_s.at[0], rel_r.at[0], yup),
              rcopy(csum.at[pl.ds(96, 96)], rrel.at[1], rel_s.at[0], rel_r.at[1], ydn)]
    top, low_half = pl.ds(0, 96), pl.ds(96, 96)

    def fin_copy(j, early):
        rows = (low_half if early else top) if j == 0 else (top if early else low_half)
        n = 2 * j + (0 if early else 1)
        return rcopy(fin.at[j, rows], rfin.at[j, rows], fin_s.at[0], fin_r.at[n],
                     yup if j == 0 else ydn)

    fin_cp = [fin_copy(j, early) for j in (0, 1) for early in (True, False)]

    def cand_cp(d):
        return rcopy(cb.at[0], cb.at[d], cb_s.at[0], cb_r.at[0], dev(x * NZ + (z + d) % NZ, t))

    project(0)
    pl.semaphore_wait(barrier, 7 + 32 + 3 + NX - 1)
    core_cp[0].start()
    project(1)
    core_cp[1].start()
    core_cp[0].wait_recv()
    csum[...] = part[1] + rcore[0]
    rel_cp[0].start()
    rel_cp[1].start()
    small[2].wait()
    e_of = iota((64, 128), 1) // 16 * 8 + iota((64, 128), 1) % 8
    dup = jnp.where(iota((64, 128), 0) == e_of, 1.0, 0.0).astype(BF16)
    c2 = jnp.dot(cbuf[...].astype(F32).astype(BF16), dup, preferred_element_type=F32)
    cb[0] = jnp.concatenate([c2, jnp.full((4, 128), -1.0, F32)], axis=0).astype(BF16)

    for d in range(1, 8):
        cand_cp(d).start()
    project(2)
    core_cp[2].start()
    core_cp[1].wait_recv()
    fin[0, 96:192] = part[3, 96:192] + rcore[1, 96:192]
    fin_cp[0].start()
    project(3)
    core_cp[3].start()
    core_cp[2].wait_recv()
    fin[1, 0:96] = part[5, 0:96] + rcore[2, 0:96]
    fin_cp[2].start()

    rel_y = [y, (y + 3) % NY, (y + 1) % NY, (y + 2) % NY]
    for rel in range(8):
        ts = 2 * rel_y[rel // 2] + (c if rel % 2 == 0 else 1 - c)
        for h, dst in ((0, q0), (1, q1)):
            cols = pl.ds(pl.multiple_of(ts * 512 + h * 256, 256), 256)
            cp = pltpu.make_async_copy(
                qh.at[:, cols], dst.at[:, pl.ds(rel * 256, 256)], q_sem.at[h]
            )
            cp.start()

    row = iota((256, 4096), 0)
    col = iota((256, 4096), 1)
    expand[...] = jnp.where((row % 64 == col // 64) & (row < 192), 1.0, 0.0).astype(BF16)
    rel_cp[0].wait_recv()
    fin[0, 0:96] = part[3, 0:96] + rcore[1, 0:96] + rrel[0]
    fin_cp[1].start()
    rel_cp[1].wait_recv()
    fin[1, 96:192] = part[5, 96:192] + rcore[2, 96:192] + rrel[1]
    fin_cp[3].start()
    tri_r, tri_c = iota((128, 128), 0), iota((128, 128), 1)
    tri = jnp.where(
        ((tri_r // 8) % 2 == 0)
        & (tri_r // 16 * 8 + tri_r % 8 < tri_c // 16 * 8 + tri_c % 8), 1.0, 0.0
    ).astype(BF16)
    mr = iota((40, 128), 0)
    slot_of = jnp.where(mr < 16, mr, jnp.where(mr < 20, mr, jnp.where(mr < 24, mr - 4, mr - 24)))
    half_of = jnp.where(mr < 20, 0, 1)
    rowkey = (slot_of + 64 * half_of).astype(F32)
    half_lane = ((iota((1, 128), 1) // 8) % 2 * 64).astype(F32)

    def choose(d):
        cz = cb[d].astype(F32)
        eqs = []
        for k in range(NX):
            g = ((x + k) % NX * NZ + z).astype(F32)
            eqs.append(jnp.where(cz == g, 1.0, 0.0))
        ranks = jnp.dot(jnp.concatenate(eqs, axis=0).astype(BF16), tri,
                        preferred_element_type=F32)
        for k in range(NX):
            hit = jnp.sum(eqs[k], axis=0, keepdims=True)
            rank = jnp.sum(ranks[8 * k:8 * k + 8], axis=0, keepdims=True)
            key = jnp.where(hit > 0.5, rank + half_lane, -1.0)
            hotb[d, 40 * k:40 * k + 40, :] = jnp.where(rowkey == key, 1.0, 0.0).astype(BF16)

    cand_all = rcopy(cb.at[pl.ds(1, 7)], cb.at[pl.ds(1, 7)], cb_s.at[0], cb_r.at[0], zup)
    cand_all.wait_recv()
    for d in range(8):
        choose(d)
    core_cp[3].wait_recv()
    for cp in fin_cp:
        cp.wait_recv()
    pbuf[...] = part[7] + rcore[3] + rfin[0] + rfin[1]

    pt = jnp.concatenate([pbuf[pl.ds(k, 8, stride=24), :] for k in range(24)], axis=0)
    lane = iota((192, 128), 1)
    low = lane < 64
    a2 = jnp.where(low, pltpu.roll(pt, 64, 1), pt)
    a4 = jnp.concatenate([a2, a2], axis=1)
    hi = pt.astype(BF16).astype(F32)
    rest = pt - hi
    mid = rest.astype(BF16).astype(F32)
    lo = rest - mid
    g3 = jnp.concatenate(
        [jnp.where(low, hi, pltpu.roll(mid, 64, 1)), jnp.where(low, lo, 0.0)], axis=1
    ).astype(BF16)
    sq = jnp.zeros((8, 256), F32)
    for m in range(16):
        gx = jnp.dot(g3, expand[:, 256 * m:256 * m + 256], preferred_element_type=F32)
        u = jnp.sum((gx * a4).reshape(24, 8, 256), axis=0)
        ubuf32[:, 256 * m:256 * m + 256] = u
        sq = sq + u * u
    inv = lax.rsqrt(jnp.sum(sq, axis=1, keepdims=True) / 4096.0 + EPS)
    for m in range(16):
        usend[m // 2, 8 * (m % 2):8 * (m % 2) + 8, :] = (
            ubuf32[:, 256 * m:256 * m + 256] * inv
        ).astype(BF16)
    my_rows = pl.ds(pl.multiple_of(t * 16, 16), 16)
    zb[0, my_rows, :] = usend[t]

    near = (0, 1, 7, 2, 6)

    def u_cp(d, k):
        to = (t + k) % 8
        return rcopy(usend.at[to], zb.at[d, my_rows, :], u_s.at[min(d, 1)], u_r.at[near.index(d)],
                     dev(x * NZ + (z + d) % NZ, to))

    for d in near:
        for k in range(8):
            if (d, k) != (0, 0):
                u_cp(d, k).start()

    def u_all(d):
        n = 7 if d == 0 else 8
        return rcopy(zb.at[d, pl.ds(0, 16 * n)], zb.at[d, pl.ds(0, 16 * n)],
                     u_s.at[min(d, 1)], u_r.at[near.index(d)], zup)

    z_half = [rcopy(zb.at[3, pl.ds(0, 64)], zb.at[4, pl.ds(0, 64)], z_s.at[0], z_r.at[0], zup),
              rcopy(zb.at[5, pl.ds(64, 64)], zb.at[4, pl.ds(64, 64)], z_s.at[1], z_r.at[1], zdn)]
    z_far = [rcopy(zb.at[2], zb.at[3], z_s.at[2], z_r.at[2], zup),
             rcopy(zb.at[6], zb.at[5], z_s.at[3], z_r.at[3], zdn)]

    def x_cp(d, k):
        return rcopy(xs.at[d, k], r.at[0, d, k], x_s.at[0], x_r.at[d],
                     dev((x + k) % NX * NZ + z, t))

    def y_cp(d, k):
        if k == 0:
            return rcopy(r.at[0, d], r.at[2, d], y_s.at[0], y_r.at[0, d], yup)
        if k == 1:
            return rcopy(r.at[0, d], r.at[4, d], y_s.at[1], y_r.at[0, d], ydn)
        if k == 2:
            return rcopy(r.at[2, d, pl.ds(0, 2)], r.at[6, d, pl.ds(0, 2)],
                         y_s.at[2], y_r.at[1, d], yup)
        return rcopy(r.at[4, d, pl.ds(2, 2)], r.at[6, d, pl.ds(2, 2)],
                     y_s.at[2], y_r.at[1, d], ydn)

    def c_cp(d, k):
        return rcopy(r.at[2 * k, d], r.at[2 * k + 1, d], c_s.at[k], c_r.at[d], partner)

    def b_cp(d, k):
        to = (x + NX - k) % NX * NZ + (z + NZ - d) % NZ
        return rcopy(rs.at[d, k], ret.at[d, k], b_s.at[1 if d == 0 else 0], b_r.at[d], dev(to, t))

    def t_cp(k):
        to = x * NZ + (z + (2 if k < 2 else NZ - 2)) % NZ
        return rcopy(rs.at[4, k], tbuf.at[k], b_s.at[0], t_r.at[k], dev(to, t))

    def t_on(k):
        to = (x + NX - k) % NX * NZ + (z + (2 if k < 2 else NZ - 2)) % NZ
        return rcopy(tbuf.at[k], ret.at[4, k], t_s.at[0], b_r.at[4], dev(to, t))

    def own_cp():
        return pltpu.make_async_copy(rs.at[0, 0], ret.at[0, 0], b_s.at[2])

    def pack(d):
        msg = jnp.dot(hotb[d], zb[d], preferred_element_type=F32)
        r[0, d, 0] = msg[0:40].astype(BF16)
        for k in range(1, NX):
            xs[d, k] = msg[40 * k:40 * k + 40].astype(BF16)

    row8 = iota((8, 128), 0)

    def scores(d):
        l0 = jnp.concatenate([r[k, d, :, 0:24, :].reshape(96, 256) for k in range(8)], axis=1)
        l1 = jnp.concatenate([r[k, d, :, 16:40, :].reshape(96, 256) for k in range(8)], axis=1)
        acc0 = lax.dot_general(l0, q0[...], NT, preferred_element_type=F32)
        acc1 = lax.dot_general(l1, q1[...], NT, preferred_element_type=F32)
        for k in range(NX):
            b = 24 * k
            m = acc0[b:b + 16] + acc1[b + 8:b + 24]
            ex = acc0[b + 16:b + 24] + pltpu.roll(acc1[b:b + 8], 4, 0)
            ex2 = pltpu.roll(ex, 4, 0)
            for j in range(5):
                rs[d, k, 16 * j:16 * j + 16, :] = m[:, 128 * j:128 * j + 128].astype(BF16)
            for j in range(3):
                v = ex[:, 128 * j:128 * j + 128]
                if j < 2:
                    v = jnp.where(row8 < 4, v, ex2[:, 128 * j + 384:128 * j + 512])
                rs[d, k, 80 + 8 * j:88 + 8 * j, :] = v.astype(BF16)

    def s1(d):
        pack(d)
        for k in (2, 1, 3):
            x_cp(d, k).start()

    def s2(d):
        rcopy(r.at[0, d, pl.ds(1, 3)], r.at[0, d, pl.ds(1, 3)], x_s.at[0], x_r.at[d], zup).wait_recv()
        y_cp(d, 0).start()
        y_cp(d, 1).start()
        c_cp(d, 0).start()

    def s3(d):
        rcopy(r.at[pl.ds(0, 2), d], r.at[pl.ds(0, 2), d], y_s.at[0], y_r.at[0, d], zup).wait_recv()
        y_cp(d, 2).start()
        y_cp(d, 3).start()
        c_cp(d, 1).start()
        c_cp(d, 2).start()

    def s4(d):
        rcopy(r.at[6, d], r.at[6, d], y_s.at[2], y_r.at[1, d], zup).wait_recv()
        c_cp(d, 3).start()

    def s5(d):
        rcopy(r.at[pl.ds(0, 4), d], r.at[pl.ds(0, 4), d], c_s.at[0], c_r.at[d], zup).wait_recv()
        scores(d)
        for k in range(NX):
            if d == 4:
                t_cp(k).start()
            elif (d, k) == (0, 0):
                own_cp().start()
            else:
                b_cp(d, k).start()

    def u_wait(d):
        u_all(d).wait_recv()

    for d in near:
        u_wait(d)
        if d == 2:
            z_far[0].start()
        if d == 6:
            z_far[1].start()
        s1(d)
    for h, dst in ((0, q0), (1, q1)):
        pltpu.make_async_copy(qh.at[:, pl.ds(0, 2048)], dst, q_sem.at[h]).wait()
    s2(1)
    z_far[0].wait_recv()
    z_half[0].start()
    s1(3)
    z_far[1].wait_recv()
    z_half[1].start()
    s1(5)
    s2(6), s3(1), s2(3)
    z_half[0].wait_recv()
    z_half[1].wait_recv()
    s1(4)
    s3(6), s2(5)
    s4(1), s3(3), s5(1), s2(4)
    s4(6), s3(5), s2(2), s5(6)
    s4(3), s3(4), s2(7), s5(3)
    s4(5), s3(2), s2(0), s4(4), s5(5)
    s3(7), s4(2), s5(4)
    s3(0), s4(7), s5(2)
    s4(0), s5(7), s5(0)

    def relay(ks):
        for k in ks:
            t_cp(k).wait_recv()
            t_on(k).start()

    relay((2, 3, 0, 1))

    def sent():
        rcopy(rcore, rcore, core_s.at[0], core_r.at[0], zup).wait_send()
        rcopy(fin, fin, fin_s.at[0], fin_r.at[0], zup).wait_send()
        rcopy(csum, csum, rel_s.at[0], rel_r.at[0], zup).wait_send()
        for j in range(2):
            z_half[j].wait_send()
        u_all(0).wait_send()
        rcopy(zb.at[pl.ds(0, 4)], zb.at[pl.ds(0, 4)], u_s.at[1], u_r.at[0], zup).wait_send()
        cand_all.wait_send()
        for cp in z_far:
            cp.wait_send()

        rcopy(xs.at[:, pl.ds(1, 3)], xs.at[:, pl.ds(1, 3)], x_s.at[0], x_r.at[0], zup).wait_send()
        for k in range(3):
            rcopy(r.at[k], r.at[k], y_s.at[k], y_r.at[0, 0], zup).wait_send()
        for k in range(4):
            rcopy(r.at[k], r.at[k], c_s.at[k], c_r.at[0], zup).wait_send()

    sent()

    def got(d):
        if d == 0:
            own_cp().wait()
            some = ret.at[0, pl.ds(1, 3)]
        else:
            some = ret.at[d]
        rcopy(some, some, b_s.at[0], b_r.at[d], zup).wait_recv()

    for d in (1, 6, 3, 5, 2, 7, 0, 4):
        got(d)

    def returned():
        some = rs.at[pl.ds(1, 7)]
        rcopy(some, some, b_s.at[0], b_r.at[1], zup).wait_send()
        some = rs.at[0, pl.ds(1, 3)]
        rcopy(some, some, b_s.at[1], b_r.at[0], zup).wait_send()
        rcopy(tbuf, tbuf, t_s.at[0], t_r.at[0], zup).wait_send()

    returned()


def pick_kernel(cand, ret, out):
    dp = lax.axis_index("dp")
    cd = cand[...]
    rel = ((cd % NZ - dp % NZ + NZ) % NZ * NX + (cd // NZ - dp // NZ + NX) % NX).astype(F32)
    group = iota((32, 64), 0).astype(F32)
    hit = jnp.zeros((32, 64), F32)
    for k in range(4):
        hit = hit + jnp.where(rel[k:k + 1, :] == group, 1.0, 0.0)
    tri = jnp.where(iota((64, 256), 0) < iota((64, 256), 1) % 64, 1.0, 0.0).astype(BF16)
    rank = jnp.dot(hit.astype(BF16), tri, preferred_element_type=F32)
    lane = iota((64, 256), 1)
    dup = jnp.where(iota((64, 256), 0) == lane % 64, 1.0, 0.0).astype(BF16)
    wide = jnp.dot(rel.astype(BF16), dup, preferred_element_type=F32)
    flat = jnp.sum(jnp.where(iota((4, 256), 0) == iota((4, 256), 1) // 64, wide, 0.0),
                   axis=0, keepdims=True)
    mine = jnp.where(flat == iota((32, 256), 0).astype(F32), rank, 0.0)
    slot = jnp.sum(mine, axis=0, keepdims=True)
    rows = jnp.concatenate([flat, slot, jnp.zeros((6, 256), F32)], axis=0).astype(BF16)
    eye = jnp.where(iota((8, 128), 0) == iota((8, 128), 1), 1.0, 0.0).astype(BF16)
    cols = lax.dot_general(rows, eye, (((0,), (0,)), ((), ())), preferred_element_type=F32)
    relc, slotc = cols[:, 0:1], cols[:, 1:2]
    key = jnp.where(slotc < 15.5, relc * 16.0 + slotc, -1.0)
    key0 = jnp.where(slotc > 15.5, relc * 8.0 + slotc - 16.0, -1.0)
    key1 = jnp.where(slotc > 15.5, relc * 8.0 + slotc - 12.0, -1.0)
    at512 = iota((256, 512), 1).astype(F32)
    at256 = iota((256, 256), 1).astype(F32)
    hot = jnp.where(at512 == key, 1.0, 0.0).astype(BF16)
    hot0 = jnp.where(at256 == key0, 1.0, 0.0).astype(BF16)
    hot1 = jnp.where(at256 == key1, 1.0, 0.0).astype(BF16)
    for js, more in (((0, 1, 2), hot0), ((3, 4), hot1)):
        pick = jnp.concatenate([hot, more], axis=1)
        vals = jnp.concatenate(
            [jnp.concatenate([
                ret[:, :, 16 * j:16 * j + 16, :].reshape(512, 128),
                ret[:, :, 80 + 8 * (j % 3):88 + 8 * (j % 3), :].reshape(256, 128),
            ], axis=0) for j in js], axis=1)
        res = jnp.dot(pick, vals, preferred_element_type=F32)
        for k in range(4):
            out[:, k, 128 * js[0]:128 * js[-1] + 128] = res[64 * k:64 * k + 64]


def local(activations, out_grads, proj_in, proj_out, queries, candidates):
    cand_t = candidates.T
    vm = pl.BlockSpec(memory_space=pltpu.VMEM)
    hbm = pl.BlockSpec(memory_space=pl.ANY)
    dma = pltpu.SemaphoreType.DMA
    ret = pl.pallas_call(
        main_kernel,
        name="attribution",
        out_shape=jax.ShapeDtypeStruct((8, 4, 104, 128), BF16),
        in_specs=[hbm] * 6,
        out_specs=hbm,
        scratch_shapes=[
            pltpu.VMEM((4, 384, 1792), BF16),
            pltpu.VMEM((4, 384, 512), BF16),
            pltpu.VMEM((128, 1792), BF16),
            pltpu.VMEM((128, 512), BF16),
            pltpu.VMEM((256, 4096), BF16),
            pltpu.VMEM((8, 192, 128), F32),
            pltpu.VMEM((4, 192, 128), F32),
            pltpu.VMEM((192, 128), F32),
            pltpu.VMEM((2, 96, 128), F32),
            pltpu.VMEM((2, 192, 128), F32),
            pltpu.VMEM((2, 192, 128), F32),
            pltpu.VMEM((192, 128), F32),
            pltpu.VMEM((8, 4096), F32),
            pltpu.VMEM((8, 16, 256), BF16),
            pltpu.VMEM((8, 128, 256), BF16),
            pltpu.VMEM((8, 8, 128), BF16),
            pltpu.VMEM((8, 160, 128), BF16),
            pltpu.VMEM((8, 4, 40, 256), BF16),
            pltpu.VMEM((8, 8, 4, 40, 256), BF16),
            pltpu.VMEM((640, 2048), BF16),
            pltpu.VMEM((640, 2048), BF16),
            pltpu.VMEM((8, 4, 104, 128), BF16),
            pltpu.VMEM((4, 104, 128), BF16),
            pltpu.VMEM((4, 64), I32),
            dma((4,)), dma((4,)), dma((2,)), dma((3,)),
            dma((1,)), dma((1,)), dma((1,)), dma((4,)), dma((1,)), dma((2,)), dma((1,)), dma((4,)),
            dma((2,)), dma((5,)), dma((4,)), dma((4,)), dma((1,)), dma((8,)), dma((3,)), dma((2, 8)),
            dma((4,)), dma((8,)), dma((3,)), dma((8,)), dma((1,)), dma((4,)),
        ],
        compiler_params=pltpu.CompilerParams(
            collective_id=0, has_side_effects=True, vmem_limit_bytes=56 * 1024 * 1024
        ),
    )(
        activations.reshape(1536, 1792), out_grads.reshape(1536, 512),
        proj_in.T, proj_out.T, queries[0], cand_t,
    )
    return pl.pallas_call(
        pick_kernel,
        name="pick",
        out_shape=jax.ShapeDtypeStruct((64, 4, 640), F32),
        in_specs=[vm, vm],
        out_specs=vm,
    )(cand_t, ret)


def solution(mesh):
    placed = (
        P("dp", None, "tensor"),
        P("dp", None, "tensor"),
        P("tensor", None),
        P("tensor", None),
        P("dp", "tensor", None),
        P("dp", None),
    )
    return jax.shard_map(
        local, mesh=mesh, in_specs=placed, out_specs=P("dp", None, "tensor"), check_vma=False
    )
```
